32 devices in a mesh: groups: 2 (over y), rows: 4 (over z), cols: 2 (over x), sub: 2 (over core).
Axes of the slice: x: 2, y: 2, z: 4, core: 2. Of those that a mesh axis runs over, the one named last changes fastest.
Arguments:
- trace: float32 [8, 4096, 32], P(('cols', 'sub'), 'groups', 'rows'), parts along dimension 1, may hold values from -6 to 6
Outputs:
- quotient: float32 [4, 2048, 128], P('groups', ('rows', 'cols', 'sub')), parts along dimension 0
The draws below stay inside these ranges and needn't reach their ends.
There are 2 independent parts, one for each index of `groups`. The reference program is written for one: setup_inputs(seed, part) draws one part's arguments, and reference() takes and returns one part's arrays. A program takes and returns all parts, laid end to end along the dimension named above; each array names one. Nothing has to cross between parts.
All inputs are finite; a program needn't handle non-finite values.
Results may differ from the reference program's by a relative error of at most 0.00011.
Values sent between devices are 32-bit elements; how exact they have to be, the bound alone decides.
A program may use at most 64 MiB of HBM per device.

```python
import math
import jax
import jax.numpy as jnp
from jax import lax

COLUMNS = 8
SLOW = 2048
FAST = 32


def block_scale(rng, shape, pieces, least, largest):
    def one(axis_at, blocks):
        heights = jax.random.uniform(jax.random.fold_in(jax.random.fold_in(rng, 6), axis_at), (blocks,), jnp.float32, least / len(pieces), largest / len(pieces))
        return jnp.repeat(jnp.exp(heights), shape[axis_at] // blocks).reshape((-1,) + (1,) * (len(shape) - axis_at - 1))

    level = one(*pieces[0])
    for cut in pieces[1:]:
        level = level * one(*cut)
    return level


def scatter_about(key, shape, width, most, pieces=(), kind=jnp.bfloat16):
    values = width * jax.random.normal(key, shape, jnp.float32)
    if pieces:
        values = values * block_scale(key, shape, pieces, -0.22, 0.18)
    return jnp.clip(values, -most, most).astype(kind)


def setup_inputs(seed: int = 0, part: int = 0) -> dict:
    keys = jax.random.split(jax.random.key(seed), 2)
    own_keys = jax.random.split(jax.random.fold_in(keys[1], part), 2)
    trace = scatter_about(own_keys[0], (COLUMNS, SLOW, FAST), 1.0, 6.0, ((0, 4), (2, 4)), jnp.float32)
    return {"trace": trace}


def reference(trace):
    all_cols, slow_len, fast_len = trace.shape
    trace_len = slow_len * fast_len
    ext_len = 4 * trace_len
    values = trace.reshape(all_cols, trace_len)
    coeffs = jnp.fft.ifft(values, axis=1)
    positions = jnp.arange(trace_len, dtype=jnp.float32) * (math.pi / (4.0 * trace_len))
    coset_shift = lax.complex(jnp.cos(positions), jnp.sin(positions))
    coeffs = jnp.pad(coeffs * coset_shift[None, :], ((0, 0), (0, ext_len - trace_len)))
    evaluations = jnp.fft.fft(coeffs, axis=1)
    wire_a = evaluations[0]
    wire_b = evaluations[1]
    wire_c = evaluations[2]
    select_mul = evaluations[3]
    select_left = evaluations[4]
    select_right = evaluations[5]
    select_out = evaluations[6]
    select_const = evaluations[7]
    gate = select_mul * wire_a * wire_b * wire_c + select_left * wire_a + select_right * wire_b + select_out * wire_c + select_const
    quarter = (jnp.arange(ext_len, dtype=jnp.int32) % 4).astype(jnp.float32)
    vanish_angle = math.pi / 4.0 - math.pi / 2.0 * quarter
    vanish = lax.complex(jnp.cos(vanish_angle) - 1.0, jnp.sin(vanish_angle))
    ratio = gate / vanish
    spread = jnp.fft.ifft(ratio) * math.sqrt(ext_len)
    ext_positions = jnp.arange(ext_len, dtype=jnp.float32) * (-math.pi / (4.0 * trace_len))
    unshift = lax.complex(jnp.cos(ext_positions), jnp.sin(ext_positions))
    result = (spread * unshift).reshape(4 * fast_len, slow_len).T
    return jnp.stack([jnp.real(result), jnp.imag(result)])
```

```python
from functools import partial
import math

import jax
import jax.numpy as jnp
import numpy as np
from jax import lax
from jax.experimental import pallas as pl
from jax.experimental.pallas import tpu as pltpu
from jax.sharding import PartitionSpec as P


def dft_table(extent, orient):
    points = jnp.arange(extent, dtype=jnp.int32)
    product = points[:, None] * points[None, :] % extent
    angles = product.astype(jnp.float32) * (orient * 2.0 * math.pi / extent)
    return (jnp.cos(angles), jnp.sin(angles))


def complex_apply(table_real, table_imag, data_real, data_imag):
    matmul = partial(jnp.dot, precision=lax.Precision.HIGHEST, preferred_element_type=jnp.float32)
    out_real = matmul(table_real, data_real) - matmul(table_imag, data_imag)
    out_imag = matmul(table_real, data_imag) + matmul(table_imag, data_real)
    return (out_real, out_imag)


def rotate(data_real, data_imag, angles):
    cosine = jnp.cos(angles)
    sine = jnp.sin(angles)
    return (data_real * cosine - data_imag * sine, data_real * sine + data_imag * cosine)


def turn(index_product, modulus, orient):
    return (index_product % modulus).astype(jnp.float32) * (orient * 2.0 * math.pi / modulus)


def transform_lead(data_real, data_imag, orient):
    extent = data_real.shape[0]
    rest_shape = data_real.shape[1:]
    breadth = data_real.size // extent
    flat_real = data_real.reshape(extent, breadth)
    flat_imag = data_imag.reshape(extent, breadth)
    if extent <= 128:
        table_real, table_imag = dft_table(extent, orient)
        out_real, out_imag = complex_apply(table_real, table_imag, flat_real, flat_imag)
    else:
        outer_len = extent // 128
        first_real, first_imag = transform_lead(
            flat_real.reshape(outer_len, 128 * breadth),
            flat_imag.reshape(outer_len, 128 * breadth),
            orient,
        )
        first_real = first_real.reshape(outer_len, 128, breadth)
        first_imag = first_imag.reshape(outer_len, 128, breadth)
        outer_index = jnp.arange(outer_len, dtype=jnp.int32)[:, None]
        inner_index = jnp.arange(128, dtype=jnp.int32)[None, :]
        angles = turn(outer_index * inner_index, extent, orient)[:, :, None]
        first_real, first_imag = rotate(first_real, first_imag, angles)
        first_real = jnp.transpose(first_real, (1, 0, 2)).reshape(128, outer_len * breadth)
        first_imag = jnp.transpose(first_imag, (1, 0, 2)).reshape(128, outer_len * breadth)
        out_real, out_imag = transform_lead(first_real, first_imag, orient)
    return (out_real.reshape((extent,) + rest_shape), out_imag.reshape((extent,) + rest_shape))


def times(first, second):
    return (
        first[0] * second[0] - first[1] * second[1],
        first[0] * second[1] + first[1] * second[0],
    )


def plus(first, second):
    return (first[0] + second[0], first[1] + second[1])


def on_device(trace):
    local_cols = trace.shape[0]
    slow_len = trace.shape[1]
    fast_local = trace.shape[2]
    row_parts = lax.axis_size("rows")
    group_parts = lax.axis_size(("cols", "sub"))
    row_index = lax.axis_index("rows")
    group_index = lax.axis_index(("cols", "sub"))
    fast_len = fast_local * row_parts
    trace_len = slow_len * fast_len
    ext_len = 4 * trace_len
    ext_slow = 4 * fast_len
    slow_block = slow_len // row_parts
    ext_block = ext_slow // row_parts
    point_block = ext_block // group_parts
    coeff_block = slow_block // group_parts
    real_part = jnp.transpose(trace, (1, 0, 2))
    imag_part = jnp.zeros_like(real_part)
    real_part, imag_part = transform_lead(real_part, imag_part, 1.0)
    lead_index = jnp.arange(slow_len, dtype=jnp.int32)[:, None, None]
    fast_index = (row_index * fast_local + jnp.arange(fast_local, dtype=jnp.int32))[None, None, :]
    real_part, imag_part = rotate(
        real_part, imag_part, turn(lead_index * fast_index, trace_len, 1.0)
    )
    moved = lax.all_to_all(
        jnp.stack([real_part, imag_part]), "rows", split_axis=1, concat_axis=3, tiled=True
    )
    moved = jnp.transpose(moved, (0, 3, 2, 1))
    real_part, imag_part = transform_lead(moved[0], moved[1], 1.0)
    slow_index = (row_index * slow_block + jnp.arange(slow_block, dtype=jnp.int32))[None, None, :]
    coeff_index = jnp.arange(fast_len, dtype=jnp.int32)[:, None, None] * slow_len + slow_index
    shift_angle = coeff_index.astype(jnp.float32) * (math.pi / (4.0 * trace_len))
    real_part, imag_part = rotate(real_part / trace_len, imag_part / trace_len, shift_angle)
    padding = jnp.zeros((ext_slow - fast_len, local_cols, slow_index.shape[2]), jnp.float32)
    real_part = jnp.concatenate([real_part, padding], 0)
    imag_part = jnp.concatenate([imag_part, padding], 0)
    real_part, imag_part = transform_lead(real_part, imag_part, -1.0)
    ext_index = jnp.arange(ext_slow, dtype=jnp.int32)[:, None, None]
    real_part, imag_part = rotate(real_part, imag_part, turn(ext_index * slow_index, ext_len, -1.0))
    stacked = jnp.stack([real_part, imag_part])
    moved = lax.all_to_all(stacked, "rows", split_axis=1, concat_axis=3, tiled=True)
    moved = jnp.transpose(moved, (0, 3, 2, 1))
    real_part, imag_part = transform_lead(moved[0], moved[1], -1.0)
    joined = lax.all_to_all(
        jnp.stack([real_part, imag_part]), ("cols", "sub"), split_axis=3, concat_axis=2, tiled=True
    )
    real_part = joined[0]
    imag_part = joined[1]

    def column(number):
        return (real_part[:, number], imag_part[:, number])

    wire_a = column(0)
    wire_b = column(1)
    wire_c = column(2)
    gate = times(times(times(column(3), wire_a), wire_b), wire_c)
    gate = plus(gate, times(column(4), wire_a))
    gate = plus(gate, times(column(5), wire_b))
    gate = plus(gate, times(column(6), wire_c))
    gate = plus(gate, column(7))
    point_index = (
        row_index * ext_block + group_index * point_block + jnp.arange(point_block, dtype=jnp.int32)
    )
    quarter = (point_index % 4).astype(jnp.float32)
    vanish_angle = math.pi / 4.0 - math.pi / 2.0 * quarter
    vanish_real = (jnp.cos(vanish_angle) - 1.0)[None, :]
    vanish_imag = jnp.sin(vanish_angle)[None, :]
    magnitude = vanish_real * vanish_real + vanish_imag * vanish_imag
    ratio_real = (gate[0] * vanish_real + gate[1] * vanish_imag) / magnitude
    ratio_imag = (gate[1] * vanish_real - gate[0] * vanish_imag) / magnitude
    real_part, imag_part = transform_lead(ratio_real, ratio_imag, 1.0)
    freq_index = jnp.arange(slow_len, dtype=jnp.int32)[:, None]
    real_part, imag_part = rotate(
        real_part, imag_part, turn(freq_index * point_index[None, :], ext_len, 1.0)
    )
    moved = lax.all_to_all(
        lax.all_to_all(
            jnp.stack([real_part, imag_part]), "rows", split_axis=1, concat_axis=2, tiled=True
        ),
        ("cols", "sub"),
        split_axis=1,
        concat_axis=2,
        tiled=True,
    )
    moved = moved.reshape(2, coeff_block, group_parts, row_parts, point_block)
    moved = jnp.transpose(moved, (0, 3, 2, 4, 1)).reshape(2, ext_slow, coeff_block)
    real_part, imag_part = transform_lead(moved[0], moved[1], 1.0)
    low_index = (
        row_index * slow_block
        + group_index * coeff_block
        + jnp.arange(coeff_block, dtype=jnp.int32)
    )[None, :]
    final_index = jnp.arange(ext_slow, dtype=jnp.int32)[:, None] * slow_len + low_index
    final_angle = final_index.astype(jnp.float32) * (-math.pi / (4.0 * trace_len))
    real_part, imag_part = rotate(real_part, imag_part, final_angle)
    result = jnp.stack([real_part, imag_part]) * (1.0 / math.sqrt(ext_len))
    return jnp.transpose(result, (0, 2, 1))


MESH = pl.DeviceIdType.MESH
CHUNKS = 2


def halves(table):
    high = table.astype(jnp.bfloat16)
    low = (table - high.astype(np.float64)).astype(jnp.bfloat16)
    return high, low


def fused_tables(sizes):
    side, fast_len, fast_local, rows, groups, blocks = sizes
    points = side * side
    ext = rows * points
    low_len = side // fast_len
    slow_len = side * low_len
    index = np.arange(side)
    angles = 2.0 * np.pi * (index[:, None] * index[None, :] % side) / side
    dft = np.stack(halves(np.cos(angles)) + halves(np.sin(angles)))
    lane_row, lane_low, lane_fast = np.meshgrid(
        np.arange(rows), np.arange(low_len), np.arange(fast_local), indexing="ij"
    )
    inner = (fast_len * lane_low + fast_local * lane_row + lane_fast).reshape(-1)
    theta = 2.0 * np.pi * (index[:, None] - side // 2) * inner[None, :] / points
    base = np.stack([np.cos(theta), np.sin(theta)]).astype(np.float32)
    shifts = 0.5 / rows - np.arange(rows) / rows
    kernels = []
    for shift in shifts:
        gap = inner[:, None] - inner[None, :] + shift
        sign = 1.0 - 2.0 * (inner[None, :] % 2)
        kernels.append(
            np.stack(
                halves(sign / points * np.sin(np.pi * shift) / np.sin(np.pi * gap / side))
            )
        )
    kernels = np.stack(kernels)
    low_index = np.repeat(np.arange(low_len), fast_local)
    spin = 2.0 * np.pi * low_index[:, None] * index[None, :] / slow_len
    spin = np.stack([np.cos(spin), np.sin(spin)]).astype(np.float32)
    source_row, source_group, fast_at = np.meshgrid(
        np.arange(rows), np.arange(groups), np.arange(fast_local), indexing="ij"
    )
    low_digit = rows * (fast_local * source_group + fast_at) + source_row
    vanish = np.exp(1j * (np.pi / rows - 2.0 * np.pi / rows * source_row)) - 1.0
    finals = np.arange(rows * fast_len)
    turns = np.exp(
        2j * np.pi * low_digit[..., None] * finals / (rows * fast_len)
        - 1j * np.pi * slow_len * finals / ext
    ) / (vanish[..., None] * math.sqrt(ext))
    real_rows = np.concatenate([turns.real, turns.imag], -1)
    imag_rows = np.concatenate([-turns.imag, turns.real], -1)
    final = np.stack([real_rows, imag_rows], 2).reshape(-1, 2 * rows * fast_len)
    final = np.stack(halves(final))
    return dft, kernels, base, spin, final


def split(value):
    high = value.astype(jnp.bfloat16)
    return high, (value - high.astype(jnp.float32)).astype(jnp.bfloat16)


def dot3(left, right):
    mul = partial(jnp.dot, preferred_element_type=jnp.float32)
    return mul(left[0], right[0]) + (mul(left[0], right[1]) + mul(left[1], right[0]))


def short_transform(values):
    count = len(values)
    if count == 1:
        return values
    even = short_transform(values[0::2])
    odd = short_transform(values[1::2])
    first, second = [], []
    for at in range(count // 2):
        cosine = math.cos(2.0 * math.pi * at / count)
        sine = math.sin(2.0 * math.pi * at / count)
        real, imag = odd[at]
        if at == 0:
            spun = (real, imag)
        elif 4 * at == count:
            spun = (-imag, real)
        else:
            spun = (real * cosine - imag * sine, real * sine + imag * cosine)
        first.append(plus(even[at], spun))
        second.append((even[at][0] - spun[0], even[at][1] - spun[1]))
    return first + second


def fused_kernel(
    sizes,
    x_ref,
    dft_hbm,
    kern_hbm,
    base_hbm,
    spin_hbm,
    final_hbm,
    out_ref,
    dft,
    kern,
    base,
    spin,
    final,
    gathered,
    staged,
    total,
    data_high,
    data_low,
    wide_high,
    wide_low,
    send_block,
    recv_block,
    send_tail,
    recv_tail,
    post,
    twist,
    table_sem,
    gather_send,
    gather_recv,
    block_send,
    block_recv,
    tail_send,
    tail_recv,
):
    side, fast_len, fast_local, rows, groups, (cols, subs) = sizes
    points = side * side
    ext = rows * points
    low_len = side // fast_len
    half = low_len * fast_local
    wide = 2 * half
    piece = side // CHUNKS
    members = rows * groups
    row = lax.axis_index("rows")
    col = lax.axis_index("cols")
    sub = lax.axis_index("sub")
    group = col * subs + sub
    me = row * groups + group

    def place(member):
        inside = lax.rem(member, groups)
        return {
            "rows": lax.div(member, groups),
            "cols": lax.div(inside, subs),
            "sub": lax.rem(inside, subs),
        }

    barrier = pltpu.get_barrier_semaphore()
    for step in range(1, members):
        pl.semaphore_signal(
            barrier, inc=1, device_id=place(lax.rem(me + step, members)), device_id_type=MESH
        )
    loads = [
        pltpu.make_async_copy(dft_hbm, dft, table_sem.at[0]),
        pltpu.make_async_copy(base_hbm, base, table_sem.at[1]),
        pltpu.make_async_copy(kern_hbm.at[row], kern, table_sem.at[2]),
        pltpu.make_async_copy(spin_hbm, spin, table_sem.at[3]),
        pltpu.make_async_copy(final_hbm, final, table_sem.at[4]),
    ]
    for load in loads:
        load.start()
    pl.semaphore_wait(barrier, members - 1)

    def hop(source, slot, chunk, way, target):
        span = pl.ds(chunk * piece, piece)
        return pltpu.make_async_remote_copy(
            src_ref=source.at[span],
            dst_ref=gathered.at[slot, span],
            send_sem=gather_send.at[slot, chunk, way],
            recv_sem=gather_recv.at[slot, chunk],
            device_id={"rows": target},
            device_id_type=MESH,
        )

    for chunk in range(CHUNKS):

        @pl.when(row < rows - 1)
        def _():
            hop(x_ref, row, chunk, 0, row + 1).start()

        @pl.when(row > 0)
        def _():
            hop(x_ref, row, chunk, 1, row - 1).start()

    lane = lax.broadcasted_iota(jnp.int32, (side, wide), 1)
    left = lane < half
    sign = jnp.where(left, -1.0, 1.0)

    def first_stage(block, slot):
        data = split(block)
        cosines = dot3((dft[0], dft[1]), data)
        sines = dot3((dft[2], dft[3]), data)
        staged[slot] = cosines + sign * pltpu.roll(sines, half, 1)
        return jnp.sum(block.reshape(side // 8, 8, wide), 0)

    shift = 0.5 / rows - row.astype(jnp.float32) / rows
    loads[0].wait()
    total[...] = first_stage(x_ref[...], row)
    high_index = lax.broadcasted_iota(jnp.int32, (side, side), 0).astype(jnp.float32)
    angle = (high_index - side // 2) * (shift * (2.0 * math.pi / points))
    turn_cos = jnp.cos(angle)
    turn_sin = jnp.sin(angle)
    loads[1].wait()
    post[0] = base[0] * turn_cos + base[1] * turn_sin
    post[1] = base[0] * turn_sin - base[1] * turn_cos
    at_row = lax.broadcasted_iota(jnp.int32, (half, side), 0)
    at_lane = lax.broadcasted_iota(jnp.int32, (half, side), 1)
    low_freq = at_lane + side * (at_row // fast_local)
    digit = rows * (fast_local * group + at_row % fast_local) + row
    tail_angle = ((low_freq * (2 * digit - 1)) % (2 * ext)).astype(jnp.float32) * (math.pi / ext)
    twist[0] = jnp.cos(tail_angle)
    twist[1] = jnp.sin(tail_angle)

    @pl.loop(0, rows - 1)
    def _(step):
        inner = jnp.where(
            step == 0, row - 1, jnp.where(step == 1, row + 1, 2 * rows - 2 - 3 * row)
        )
        slot = jnp.where(
            row == 0, step + 1, jnp.where(row == rows - 1, rows - 2 - step, inner)
        )
        for chunk in range(CHUNKS):
            hop(x_ref, slot, chunk, 0, row).wait_recv()

            @pl.when((slot < row) & (row < rows - 1))
            def _():
                hop(gathered.at[slot], slot, chunk, 0, row + 1).start()

            @pl.when((slot > row) & (row > 0))
            def _():
                hop(gathered.at[slot], slot, chunk, 1, row - 1).start()

        total[...] += first_stage(gathered[slot], slot)

    sums = jnp.sum(total[...], 0, keepdims=True)
    narrow = lax.broadcasted_iota(jnp.int32, (1, wide), 1) < half
    mean_a = jnp.sum(jnp.where(narrow, sums, 0.0), 1, keepdims=True) * (1.0 / points)
    mean_b = jnp.sum(jnp.where(narrow, 0.0, sums), 1, keepdims=True) * (1.0 / points)

    for pair in range(rows // 2):
        first = staged[2 * pair]
        second = staged[2 * pair + 1]
        real = jnp.where(left, first, pltpu.roll(second, half, 1))
        imag = jnp.where(left, pltpu.roll(first, half, 1), second)
        span = slice(pair * wide, (pair + 1) * wide)
        cosine = base[0, :, span]
        sine = base[1, :, span]
        high, low = split(real * cosine - imag * sine)
        data_high[:side, span] = high
        data_low[:side, span] = low
        high, low = split(real * sine + imag * cosine)
        data_high[side:, span] = high
        data_low[side:, span] = low
    loads[2].wait()
    moved = dot3((data_high[...], data_low[...]), (kern[0], kern[1]))
    real = moved[:side]
    imag = moved[side:]
    new_real = real * post[0] - imag * post[1]
    new_imag = real * post[1] + imag * post[0]
    half_turn = jnp.zeros((1, 1), jnp.float32) + shift * math.pi
    half_cos = jnp.cos(half_turn)
    half_sin = jnp.sin(half_turn)
    row_at = lax.broadcasted_iota(jnp.int32, (side, side), 0)
    lane_at = lax.broadcasted_iota(jnp.int32, (side, side), 1)
    parity = jnp.where(row_at == 0, (1 - 2 * (lane_at % 2)).astype(jnp.float32), 0.0)
    new_real = new_real - parity * (mean_a * half_cos + mean_b * half_sin)
    new_imag = new_imag - parity * (mean_b * half_cos - mean_a * half_sin)
    high, low = split(new_real)
    wide_high[:side] = high
    wide_low[:side] = low
    high, low = split(new_imag)
    wide_high[side:] = high
    wide_low[side:] = low

    means = jnp.broadcast_to(jnp.where(narrow, mean_a, mean_b), (8, wide))

    def block_copy(target):
        return pltpu.make_async_remote_copy(
            src_ref=send_block.at[target],
            dst_ref=recv_block.at[group],
            send_sem=block_send.at[target],
            recv_sem=block_recv.at[group],
            device_id={"cols": lax.div(target, subs), "sub": lax.rem(target, subs)},
            device_id_type=MESH,
        )

    def block_arrival(source):
        return pltpu.make_async_remote_copy(
            src_ref=send_block.at[source],
            dst_ref=recv_block.at[source],
            send_sem=block_send.at[source],
            recv_sem=block_recv.at[source],
            device_id={"cols": lax.div(source, subs), "sub": lax.rem(source, subs)},
            device_id_type=MESH,
        )

    @pl.loop(0, cols)
    def _(step):
        tile = lax.rem(col + 1 + step, cols)
        span = pl.ds(pl.multiple_of(tile * wide, wide), wide)
        upper = (wide_high[:side, span], wide_low[:side, span])
        lower = (wide_high[side:, span], wide_low[side:, span])
        cosine = (dft[0], dft[1])
        sine = (dft[2], dft[3])
        value_a = dot3(cosine, upper) + dot3(sine, lower)
        value_b = dot3(cosine, lower) - dot3(sine, upper)
        send_block[tile * subs, :side] = jnp.where(left, value_a, pltpu.roll(value_b, half, 1))
        send_block[tile * subs + 1, :side] = jnp.where(
            left, pltpu.roll(value_a, half, 1), value_b
        )
        for at in range(2):
            send_block[tile * subs + at, side:] = means

            @pl.when(tile * subs + at != group)
            def _():
                block_copy(tile * subs + at).start()

    recv_block[group] = send_block[group]
    for step in range(1, groups):
        block_arrival(lax.rem(group + step, groups)).wait_recv()

    spin_cos = jnp.cos(half_turn)
    spin_sin = jnp.sin(half_turn)
    flip = (1 - 2 * (lane % 2)).astype(jnp.float32)
    part_cos = flip * spin_cos
    part_sin = flip * spin_sin

    def value(number):
        data = recv_block[number, :side]
        mean = recv_block[number, side : side + 1]
        return (mean + part_cos * data, part_sin * data)

    def swap(pair):
        return (pltpu.roll(pair[0], half, 1), pltpu.roll(pair[1], half, 1))

    block_ab = value(0)
    block_cm = value(1)
    block_qab = value(2)
    block_qck = value(3)
    cubic = times(block_ab, block_cm)
    linear = times(block_ab, block_qab)
    gate = times(cubic, swap(cubic))
    gate = plus(gate, plus(linear, swap(linear)))
    gate = plus(gate, times(block_cm, block_qck))
    gate = plus(gate, swap(block_qck))
    packed = jnp.where(left, gate[0], pltpu.roll(gate[1], half, 1))
    turned = split(jnp.transpose(packed))
    cosines = dot3(turned, (dft[0], dft[1]))
    sines = dot3(turned, (dft[2], dft[3]))
    real = cosines[:half] - sines[half:]
    imag = cosines[half:] + sines[:half]
    loads[3].wait()
    loads[4].wait()
    real, imag = (real * spin[0] - imag * spin[1], real * spin[1] + imag * spin[0])
    values = [
        (real[at * fast_local : (at + 1) * fast_local], imag[at * fast_local : (at + 1) * fast_local])
        for at in range(low_len)
    ]
    values = short_transform(values)
    tails = members // low_len
    breadth = side // tails
    for at in range(low_len):
        rows_at = slice(at * fast_local, (at + 1) * fast_local)
        real, imag = values[at]
        cosine = twist[0, rows_at]
        sine = twist[1, rows_at]
        out_real = real * cosine - imag * sine
        out_imag = real * sine + imag * cosine
        for part in range(tails):
            lanes = slice(part * breadth, (part + 1) * breadth)
            send_tail[at * tails + part, :fast_local] = out_real[:, lanes]
            send_tail[at * tails + part, fast_local:] = out_imag[:, lanes]

    def tail_copy(target, slot):
        return pltpu.make_async_remote_copy(
            src_ref=send_tail.at[target],
            dst_ref=recv_tail.at[slot],
            send_sem=tail_send.at[target],
            recv_sem=tail_recv.at[slot],
            device_id=place(target),
            device_id_type=MESH,
        )

    for step in range(1, members):
        tail_copy(lax.rem(me + step, members), me).start()
    recv_tail[me] = send_tail[me]
    for step in range(1, members):
        source = lax.rem(me + step, members)
        tail_copy(source, source).wait_recv()
    flat = recv_tail[...].reshape(members * 2 * fast_local, breadth)
    result = dot3(split(jnp.transpose(flat)), (final[0], final[1]))
    out_ref[0] = result[:, : rows * fast_len]
    out_ref[1] = result[:, rows * fast_len :]

    for step in range(1, members):
        target = lax.rem(me + step, members)
        tail_copy(target, me).wait_send()
    for step in range(1, groups):
        block_copy(lax.rem(group + step, groups)).wait_send()
    for chunk in range(CHUNKS):
        for slot in range(rows):

            @pl.when((slot <= row) & (row < rows - 1))
            def _():
                hop(x_ref, slot, chunk, 0, row + 1).wait_send()

            @pl.when((slot >= row) & (row > 0))
            def _():
                hop(x_ref, slot, chunk, 1, row - 1).wait_send()


def fused_on_device(sizes, trace):
    side, fast_len, fast_local, rows, groups, _ = sizes
    local_cols = trace.shape[0]
    low_len = side // fast_len
    half = low_len * fast_local
    wide = 2 * half
    members = rows * groups
    tables = [jnp.asarray(table) for table in fused_tables(sizes)]
    block = jnp.transpose(trace.reshape(local_cols, side, low_len, fast_local), (1, 0, 2, 3))
    block = block.reshape(side, wide)
    vmem = pltpu.VMEM
    bf16 = jnp.bfloat16
    f32 = jnp.float32
    dma = pltpu.SemaphoreType.DMA
    breadth = side * low_len // members
    return pl.pallas_call(
        partial(fused_kernel, sizes),
        out_shape=jax.ShapeDtypeStruct((2, breadth, rows * fast_len), f32),
        in_specs=[pl.BlockSpec(memory_space=vmem)]
        + [pl.BlockSpec(memory_space=pl.ANY)] * len(tables),
        out_specs=pl.BlockSpec(memory_space=vmem),
        scratch_shapes=[
            vmem((4, side, side), bf16),
            vmem((2, side, side), bf16),
            vmem((2, side, side), f32),
            vmem((2, half, side), f32),
            vmem((2, members * 2 * fast_local, 2 * rows * fast_len), bf16),
            vmem((rows, side, wide), f32),
            vmem((rows, side, wide), f32),
            vmem((8, wide), f32),
            vmem((2 * side, side), bf16),
            vmem((2 * side, side), bf16),
            vmem((2 * side, side), bf16),
            vmem((2 * side, side), bf16),
            vmem((groups, side + 8, wide), f32),
            vmem((groups, side + 8, wide), f32),
            vmem((members, 2 * fast_local, breadth), f32),
            vmem((members, 2 * fast_local, breadth), f32),
            vmem((2, side, side), f32),
            vmem((2, half, side), f32),
            dma((5,)),
            dma((rows, CHUNKS, 2)),
            dma((rows, CHUNKS)),
            dma((groups,)),
            dma((groups,)),
            dma((members,)),
            dma((members,)),
        ],
        compiler_params=pltpu.CompilerParams(collective_id=0, has_side_effects=True),
    )(block, *tables)


def fused_sizes(mesh, trace):
    shape = mesh.shape
    rows = shape["rows"]
    groups = shape["cols"] * shape["sub"]
    slow_len = trace.shape[1] // shape["groups"]
    fast_len = trace.shape[2]
    side = math.isqrt(slow_len * fast_len)
    fast_local = fast_len // rows
    local_cols = trace.shape[0] // groups
    low_len = side // fast_len
    fits = (
        side * side == slow_len * fast_len
        and low_len * fast_len == side
        and rows == 4
        and groups == rows
        and shape["cols"] == 2
        and shape["sub"] == 2
        and local_cols == 2
        and fast_local == 8
        and 2 * low_len * fast_local == 128
        and rows * groups == 2 * low_len
    )
    return (side, fast_len, fast_local, rows, groups, (shape["cols"], shape["sub"])) if fits else None


def solution(mesh):
    placed = (P(("cols", "sub"), "groups", "rows"),)

    def whole(trace):
        sizes = fused_sizes(mesh, trace)
        return jax.shard_map(
            on_device if sizes is None else partial(fused_on_device, sizes),
            mesh=mesh,
            in_specs=placed,
            out_specs=P("groups", ("rows", "cols", "sub"), None),
            check_vma=False,
        )(trace)

    return whole
```

```python
from functools import partial
import math

import jax
import jax.numpy as jnp
import numpy as np
from jax import lax
from jax.experimental import pallas as pl
from jax.experimental.pallas import tpu as pltpu
from jax.sharding import PartitionSpec as P


def dft_table(extent, orient):
    points = jnp.arange(extent, dtype=jnp.int32)
    product = points[:, None] * points[None, :] % extent
    angles = product.astype(jnp.float32) * (orient * 2.0 * math.pi / extent)
    return (jnp.cos(angles), jnp.sin(angles))


def complex_apply(table_real, table_imag, data_real, data_imag):
    matmul = partial(jnp.dot, precision=lax.Precision.HIGHEST, preferred_element_type=jnp.float32)
    out_real = matmul(table_real, data_real) - matmul(table_imag, data_imag)
    out_imag = matmul(table_real, data_imag) + matmul(table_imag, data_real)
    return (out_real, out_imag)


def rotate(data_real, data_imag, angles):
    cosine = jnp.cos(angles)
    sine = jnp.sin(angles)
    return (data_real * cosine - data_imag * sine, data_real * sine + data_imag * cosine)


def turn(index_product, modulus, orient):
    return (index_product % modulus).astype(jnp.float32) * (orient * 2.0 * math.pi / modulus)


def transform_lead(data_real, data_imag, orient):
    extent = data_real.shape[0]
    rest_shape = data_real.shape[1:]
    breadth = data_real.size // extent
    flat_real = data_real.reshape(extent, breadth)
    flat_imag = data_imag.reshape(extent, breadth)
    if extent <= 128:
        table_real, table_imag = dft_table(extent, orient)
        out_real, out_imag = complex_apply(table_real, table_imag, flat_real, flat_imag)
    else:
        outer_len = extent // 128
        first_real, first_imag = transform_lead(
            flat_real.reshape(outer_len, 128 * breadth),
            flat_imag.reshape(outer_len, 128 * breadth),
            orient,
        )
        first_real = first_real.reshape(outer_len, 128, breadth)
        first_imag = first_imag.reshape(outer_len, 128, breadth)
        outer_index = jnp.arange(outer_len, dtype=jnp.int32)[:, None]
        inner_index = jnp.arange(128, dtype=jnp.int32)[None, :]
        angles = turn(outer_index * inner_index, extent, orient)[:, :, None]
        first_real, first_imag = rotate(first_real, first_imag, angles)
        first_real = jnp.transpose(first_real, (1, 0, 2)).reshape(128, outer_len * breadth)
        first_imag = jnp.transpose(first_imag, (1, 0, 2)).reshape(128, outer_len * breadth)
        out_real, out_imag = transform_lead(first_real, first_imag, orient)
    return (out_real.reshape((extent,) + rest_shape), out_imag.reshape((extent,) + rest_shape))


def times(first, second):
    return (
        first[0] * second[0] - first[1] * second[1],
        first[0] * second[1] + first[1] * second[0],
    )


def plus(first, second):
    return (first[0] + second[0], first[1] + second[1])


def on_device(trace):
    local_cols = trace.shape[0]
    slow_len = trace.shape[1]
    fast_local = trace.shape[2]
    row_parts = lax.axis_size("rows")
    group_parts = lax.axis_size(("cols", "sub"))
    row_index = lax.axis_index("rows")
    group_index = lax.axis_index(("cols", "sub"))
    fast_len = fast_local * row_parts
    trace_len = slow_len * fast_len
    ext_len = 4 * trace_len
    ext_slow = 4 * fast_len
    slow_block = slow_len // row_parts
    ext_block = ext_slow // row_parts
    point_block = ext_block // group_parts
    coeff_block = slow_block // group_parts
    real_part = jnp.transpose(trace, (1, 0, 2))
    imag_part = jnp.zeros_like(real_part)
    real_part, imag_part = transform_lead(real_part, imag_part, 1.0)
    lead_index = jnp.arange(slow_len, dtype=jnp.int32)[:, None, None]
    fast_index = (row_index * fast_local + jnp.arange(fast_local, dtype=jnp.int32))[None, None, :]
    real_part, imag_part = rotate(
        real_part, imag_part, turn(lead_index * fast_index, trace_len, 1.0)
    )
    moved = lax.all_to_all(
        jnp.stack([real_part, imag_part]), "rows", split_axis=1, concat_axis=3, tiled=True
    )
    moved = jnp.transpose(moved, (0, 3, 2, 1))
    real_part, imag_part = transform_lead(moved[0], moved[1], 1.0)
    slow_index = (row_index * slow_block + jnp.arange(slow_block, dtype=jnp.int32))[None, None, :]
    coeff_index = jnp.arange(fast_len, dtype=jnp.int32)[:, None, None] * slow_len + slow_index
    shift_angle = coeff_index.astype(jnp.float32) * (math.pi / (4.0 * trace_len))
    real_part, imag_part = rotate(real_part / trace_len, imag_part / trace_len, shift_angle)
    padding = jnp.zeros((ext_slow - fast_len, local_cols, slow_index.shape[2]), jnp.float32)
    real_part = jnp.concatenate([real_part, padding], 0)
    imag_part = jnp.concatenate([imag_part, padding], 0)
    real_part, imag_part = transform_lead(real_part, imag_part, -1.0)
    ext_index = jnp.arange(ext_slow, dtype=jnp.int32)[:, None, None]
    real_part, imag_part = rotate(real_part, imag_part, turn(ext_index * slow_index, ext_len, -1.0))
    stacked = jnp.stack([real_part, imag_part])
    moved = lax.all_to_all(stacked, "rows", split_axis=1, concat_axis=3, tiled=True)
    moved = jnp.transpose(moved, (0, 3, 2, 1))
    real_part, imag_part = transform_lead(moved[0], moved[1], -1.0)
    joined = lax.all_to_all(
        jnp.stack([real_part, imag_part]), ("cols", "sub"), split_axis=3, concat_axis=2, tiled=True
    )
    real_part = joined[0]
    imag_part = joined[1]

    def column(number):
        return (real_part[:, number], imag_part[:, number])

    wire_a = column(0)
    wire_b = column(1)
    wire_c = column(2)
    gate = times(times(times(column(3), wire_a), wire_b), wire_c)
    gate = plus(gate, times(column(4), wire_a))
    gate = plus(gate, times(column(5), wire_b))
    gate = plus(gate, times(column(6), wire_c))
    gate = plus(gate, column(7))
    point_index = (
        row_index * ext_block + group_index * point_block + jnp.arange(point_block, dtype=jnp.int32)
    )
    quarter = (point_index % 4).astype(jnp.float32)
    vanish_angle = math.pi / 4.0 - math.pi / 2.0 * quarter
    vanish_real = (jnp.cos(vanish_angle) - 1.0)[None, :]
    vanish_imag = jnp.sin(vanish_angle)[None, :]
    magnitude = vanish_real * vanish_real + vanish_imag * vanish_imag
    ratio_real = (gate[0] * vanish_real + gate[1] * vanish_imag) / magnitude
    ratio_imag = (gate[1] * vanish_real - gate[0] * vanish_imag) / magnitude
    real_part, imag_part = transform_lead(ratio_real, ratio_imag, 1.0)
    freq_index = jnp.arange(slow_len, dtype=jnp.int32)[:, None]
    real_part, imag_part = rotate(
        real_part, imag_part, turn(freq_index * point_index[None, :], ext_len, 1.0)
    )
    moved = lax.all_to_all(
        lax.all_to_all(
            jnp.stack([real_part, imag_part]), "rows", split_axis=1, concat_axis=2, tiled=True
        ),
        ("cols", "sub"),
        split_axis=1,
        concat_axis=2,
        tiled=True,
    )
    moved = moved.reshape(2, coeff_block, group_parts, row_parts, point_block)
    moved = jnp.transpose(moved, (0, 3, 2, 4, 1)).reshape(2, ext_slow, coeff_block)
    real_part, imag_part = transform_lead(moved[0], moved[1], 1.0)
    low_index = (
        row_index * slow_block
        + group_index * coeff_block
        + jnp.arange(coeff_block, dtype=jnp.int32)
    )[None, :]
    final_index = jnp.arange(ext_slow, dtype=jnp.int32)[:, None] * slow_len + low_index
    final_angle = final_index.astype(jnp.float32) * (-math.pi / (4.0 * trace_len))
    real_part, imag_part = rotate(real_part, imag_part, final_angle)
    result = jnp.stack([real_part, imag_part]) * (1.0 / math.sqrt(ext_len))
    return jnp.transpose(result, (0, 2, 1))


MESH = pl.DeviceIdType.MESH
CHUNKS = 4


def halves(table):
    high = table.astype(jnp.bfloat16)
    low = (table - high.astype(np.float64)).astype(jnp.bfloat16)
    return high, low


def fused_tables(sizes):
    side, fast_len, fast_local, rows, groups, blocks = sizes
    points = side * side
    ext = rows * points
    low_len = side // fast_len
    slow_len = side * low_len
    index = np.arange(side)
    angles = 2.0 * np.pi * (index[:, None] * index[None, :] % side) / side
    dft = np.stack(halves(np.cos(angles)) + halves(np.sin(angles)))
    lane_row, lane_low, lane_fast = np.meshgrid(
        np.arange(rows), np.arange(low_len), np.arange(fast_local), indexing="ij"
    )
    inner = (fast_len * lane_low + fast_local * lane_row + lane_fast).reshape(-1)
    theta = 2.0 * np.pi * (index[:, None] - side // 2) * inner[None, :] / points
    base = np.stack([np.cos(theta), np.sin(theta)]).astype(np.float32)
    shifts = 0.5 / rows - np.arange(rows) / rows
    kernels = []
    for shift in shifts:
        gap = inner[:, None] - inner[None, :] + shift
        sign = 1.0 - 2.0 * (inner[None, :] % 2)
        kernels.append(
            np.stack(
                halves(sign / points * np.sin(np.pi * shift) / np.sin(np.pi * gap / side))
            )
        )
    kernels = np.stack(kernels)
    low_index = np.repeat(np.arange(low_len), fast_local)
    spin = 2.0 * np.pi * low_index[:, None] * index[None, :] / slow_len
    spin = np.stack([np.cos(spin), np.sin(spin)]).astype(np.float32)
    source_row, source_group, fast_at = np.meshgrid(
        np.arange(rows), np.arange(groups), np.arange(fast_local), indexing="ij"
    )
    low_digit = rows * (fast_local * source_group + fast_at) + source_row
    vanish = np.exp(1j * (np.pi / rows - 2.0 * np.pi / rows * source_row)) - 1.0
    finals = np.arange(rows * fast_len)
    turns = np.exp(
        2j * np.pi * low_digit[..., None] * finals / (rows * fast_len)
        - 1j * np.pi * slow_len * finals / ext
    ) / (vanish[..., None] * math.sqrt(ext))
    real_rows = np.concatenate([turns.real, turns.imag], -1)
    imag_rows = np.concatenate([-turns.imag, turns.real], -1)
    final = np.stack([real_rows, imag_rows], 2).reshape(-1, 2 * rows * fast_len)
    final = np.stack(halves(final))
    return dft, kernels, base, spin, final


def split(value):
    high = value.astype(jnp.bfloat16)
    return high, (value - high.astype(jnp.float32)).astype(jnp.bfloat16)


def dot3(left, right):
    mul = partial(jnp.dot, preferred_element_type=jnp.float32)
    return mul(left[0], right[0]) + (mul(left[0], right[1]) + mul(left[1], right[0]))


def short_transform(values):
    count = len(values)
    if count == 1:
        return values
    even = short_transform(values[0::2])
    odd = short_transform(values[1::2])
    first, second = [], []
    for at in range(count // 2):
        cosine = math.cos(2.0 * math.pi * at / count)
        sine = math.sin(2.0 * math.pi * at / count)
        real, imag = odd[at]
        if at == 0:
            spun = (real, imag)
        elif 4 * at == count:
            spun = (-imag, real)
        else:
            spun = (real * cosine - imag * sine, real * sine + imag * cosine)
        first.append(plus(even[at], spun))
        second.append((even[at][0] - spun[0], even[at][1] - spun[1]))
    return first + second


def fused_kernel(
    sizes,
    x_ref,
    dft_hbm,
    kern_hbm,
    base_hbm,
    spin_hbm,
    final_hbm,
    out_ref,
    dft,
    kern,
    base,
    spin,
    final,
    gathered,
    staged,
    total,
    data_high,
    data_low,
    wide_high,
    wide_low,
    send_block,
    recv_block,
    send_tail,
    recv_tail,
    post,
    twist,
    table_sem,
    gather_send,
    gather_recv,
    block_send,
    block_recv,
    tail_send,
    tail_recv,
):
    side, fast_len, fast_local, rows, groups, (cols, subs) = sizes
    points = side * side
    ext = rows * points
    low_len = side // fast_len
    half = low_len * fast_local
    wide = 2 * half
    piece = side // CHUNKS
    members = rows * groups
    row = lax.axis_index("rows")
    col = lax.axis_index("cols")
    sub = lax.axis_index("sub")
    group = col * subs + sub
    me = row * groups + group

    def place(member):
        inside = lax.rem(member, groups)
        return {
            "rows": lax.div(member, groups),
            "cols": lax.div(inside, subs),
            "sub": lax.rem(inside, subs),
        }

    barrier = pltpu.get_barrier_semaphore()
    for step in range(1, groups):
        other = lax.rem(group + step, groups)
        pl.semaphore_signal(
            barrier,
            inc=1,
            device_id={"cols": lax.div(other, subs), "sub": lax.rem(other, subs)},
            device_id_type=MESH,
        )

    @pl.when(row > 0)
    def _():
        pl.semaphore_signal(barrier, inc=1, device_id={"rows": row - 1}, device_id_type=MESH)

    @pl.when(row < rows - 1)
    def _():
        pl.semaphore_signal(barrier, inc=1, device_id={"rows": row + 1}, device_id_type=MESH)

    loads = [
        pltpu.make_async_copy(dft_hbm, dft, table_sem.at[0]),
        pltpu.make_async_copy(base_hbm, base, table_sem.at[1]),
        pltpu.make_async_copy(kern_hbm.at[row], kern, table_sem.at[2]),
        pltpu.make_async_copy(spin_hbm, spin, table_sem.at[3]),
        pltpu.make_async_copy(final_hbm, final, table_sem.at[4]),
    ]
    for load in loads:
        load.start()
    pl.semaphore_wait(
        barrier,
        groups - 1 + (row > 0).astype(jnp.int32) + (row < rows - 1).astype(jnp.int32),
    )

    def hop(source, slot, chunk, way, target):
        span = pl.ds(chunk * piece, piece)
        return pltpu.make_async_remote_copy(
            src_ref=source.at[span],
            dst_ref=gathered.at[slot, span],
            send_sem=gather_send.at[slot, chunk, way],
            recv_sem=gather_recv.at[slot, chunk],
            device_id={"rows": target},
            device_id_type=MESH,
        )

    for chunk in range(CHUNKS):

        @pl.when(row < rows - 1)
        def _():
            hop(x_ref, row, chunk, 0, row + 1).start()

        @pl.when(row > 0)
        def _():
            hop(x_ref, row, chunk, 1, row - 1).start()

    lane = lax.broadcasted_iota(jnp.int32, (side, wide), 1)
    left = lane < half
    sign = jnp.where(left, -1.0, 1.0)

    def first_stage(block, slot):
        data = split(block)
        cosines = dot3((dft[0], dft[1]), data)
        sines = dot3((dft[2], dft[3]), data)
        staged[slot] = cosines + sign * pltpu.roll(sines, half, 1)
        return jnp.sum(block.reshape(side // 8, 8, wide), 0)

    shift = 0.5 / rows - row.astype(jnp.float32) / rows
    loads[0].wait()
    total[...] = first_stage(x_ref[...], row)
    high_index = lax.broadcasted_iota(jnp.int32, (side, side), 0).astype(jnp.float32)
    angle = (high_index - side // 2) * (shift * (2.0 * math.pi / points))
    turn_cos = jnp.cos(angle)
    turn_sin = jnp.sin(angle)
    loads[1].wait()
    post[0] = base[0] * turn_cos + base[1] * turn_sin
    post[1] = base[0] * turn_sin - base[1] * turn_cos
    at_row = lax.broadcasted_iota(jnp.int32, (half, side), 0)
    at_lane = lax.broadcasted_iota(jnp.int32, (half, side), 1)
    low_freq = at_lane + side * (at_row // fast_local)
    digit = rows * (fast_local * group + at_row % fast_local) + row
    tail_angle = ((low_freq * (2 * digit - 1)) % (2 * ext)).astype(jnp.float32) * (math.pi / ext)
    twist[0] = jnp.cos(tail_angle)
    twist[1] = jnp.sin(tail_angle)

    @pl.loop(0, rows - 1)
    def _(step):
        inner = jnp.where(
            step == 0, row - 1, jnp.where(step == 1, row + 1, 2 * rows - 2 - 3 * row)
        )
        slot = jnp.where(
            row == 0, step + 1, jnp.where(row == rows - 1, rows - 2 - step, inner)
        )
        for chunk in range(CHUNKS):
            hop(x_ref, slot, chunk, 0, row).wait_recv()

            @pl.when((slot < row) & (row < rows - 1))
            def _():
                hop(gathered.at[slot], slot, chunk, 0, row + 1).start()

            @pl.when((slot > row) & (row > 0))
            def _():
                hop(gathered.at[slot], slot, chunk, 1, row - 1).start()

        total[...] += first_stage(gathered[slot], slot)

    sums = jnp.sum(total[...], 0, keepdims=True)
    narrow = lax.broadcasted_iota(jnp.int32, (1, wide), 1) < half
    mean_a = jnp.sum(jnp.where(narrow, sums, 0.0), 1, keepdims=True) * (1.0 / points)
    mean_b = jnp.sum(jnp.where(narrow, 0.0, sums), 1, keepdims=True) * (1.0 / points)

    for pair in range(rows // 2):
        first = staged[2 * pair]
        second = staged[2 * pair + 1]
        real = jnp.where(left, first, pltpu.roll(second, half, 1))
        imag = jnp.where(left, pltpu.roll(first, half, 1), second)
        span = slice(pair * wide, (pair + 1) * wide)
        cosine = base[0, :, span]
        sine = base[1, :, span]
        high, low = split(real * cosine - imag * sine)
        data_high[:side, span] = high
        data_low[:side, span] = low
        high, low = split(real * sine + imag * cosine)
        data_high[side:, span] = high
        data_low[side:, span] = low
    loads[2].wait()
    moved = dot3((data_high[...], data_low[...]), (kern[0], kern[1]))
    real = moved[:side]
    imag = moved[side:]
    new_real = real * post[0] - imag * post[1]
    new_imag = real * post[1] + imag * post[0]
    half_turn = jnp.zeros((1, 1), jnp.float32) + shift * math.pi
    half_cos = jnp.cos(half_turn)
    half_sin = jnp.sin(half_turn)
    row_at = lax.broadcasted_iota(jnp.int32, (side, side), 0)
    lane_at = lax.broadcasted_iota(jnp.int32, (side, side), 1)
    parity = jnp.where(row_at == 0, (1 - 2 * (lane_at % 2)).astype(jnp.float32), 0.0)
    new_real = new_real - parity * (mean_a * half_cos + mean_b * half_sin)
    new_imag = new_imag - parity * (mean_b * half_cos - mean_a * half_sin)
    high, low = split(new_real)
    wide_high[:side] = high
    wide_low[:side] = low
    high, low = split(new_imag)
    wide_high[side:] = high
    wide_low[side:] = low

    means = jnp.broadcast_to(jnp.where(narrow, mean_a, mean_b), (8, wide))

    def block_copy(target):
        return pltpu.make_async_remote_copy(
            src_ref=send_block.at[target],
            dst_ref=recv_block.at[group],
            send_sem=block_send.at[target],
            recv_sem=block_recv.at[group],
            device_id={"cols": lax.div(target, subs), "sub": lax.rem(target, subs)},
            device_id_type=MESH,
        )

    def block_arrival(source):
        return pltpu.make_async_remote_copy(
            src_ref=send_block.at[source],
            dst_ref=recv_block.at[source],
            send_sem=block_send.at[source],
            recv_sem=block_recv.at[source],
            device_id={"cols": lax.div(source, subs), "sub": lax.rem(source, subs)},
            device_id_type=MESH,
        )

    @pl.loop(0, cols)
    def _(step):
        tile = lax.rem(col + 1 + step, cols)
        span = pl.ds(pl.multiple_of(tile * wide, wide), wide)
        upper = (wide_high[:side, span], wide_low[:side, span])
        lower = (wide_high[side:, span], wide_low[side:, span])
        cosine = (dft[0], dft[1])
        sine = (dft[2], dft[3])
        value_a = dot3(cosine, upper) + dot3(sine, lower)
        value_b = dot3(cosine, lower) - dot3(sine, upper)
        send_block[tile * subs, :side] = jnp.where(left, value_a, pltpu.roll(value_b, half, 1))
        send_block[tile * subs + 1, :side] = jnp.where(
            left, pltpu.roll(value_a, half, 1), value_b
        )
        for at in range(2):
            send_block[tile * subs + at, side:] = means

            @pl.when(tile * subs + at != group)
            def _():
                block_copy(tile * subs + at).start()

    recv_block[group] = send_block[group]
    for step in range(1, groups):
        block_arrival(lax.rem(group + step, groups)).wait_recv()

    spin_cos = jnp.cos(half_turn)
    spin_sin = jnp.sin(half_turn)
    flip = (1 - 2 * (lane % 2)).astype(jnp.float32)
    part_cos = flip * spin_cos
    part_sin = flip * spin_sin

    def value(number):
        data = recv_block[number, :side]
        mean = recv_block[number, side : side + 1]
        return (mean + part_cos * data, part_sin * data)

    def swap(pair):
        return (pltpu.roll(pair[0], half, 1), pltpu.roll(pair[1], half, 1))

    block_ab = value(0)
    block_cm = value(1)
    block_qab = value(2)
    block_qck = value(3)
    cubic = times(block_ab, block_cm)
    linear = times(block_ab, block_qab)
    gate = times(cubic, swap(cubic))
    gate = plus(gate, plus(linear, swap(linear)))
    gate = plus(gate, times(block_cm, block_qck))
    gate = plus(gate, swap(block_qck))
    packed = jnp.where(left, gate[0], pltpu.roll(gate[1], half, 1))
    turned = split(jnp.transpose(packed))
    cosines = dot3(turned, (dft[0], dft[1]))
    sines = dot3(turned, (dft[2], dft[3]))
    real = cosines[:half] - sines[half:]
    imag = cosines[half:] + sines[:half]
    loads[3].wait()
    loads[4].wait()
    real, imag = (real * spin[0] - imag * spin[1], real * spin[1] + imag * spin[0])
    values = [
        (real[at * fast_local : (at + 1) * fast_local], imag[at * fast_local : (at + 1) * fast_local])
        for at in range(low_len)
    ]
    values = short_transform(values)
    tails = members // low_len
    breadth = side // tails
    for at in range(low_len):
        rows_at = slice(at * fast_local, (at + 1) * fast_local)
        real, imag = values[at]
        cosine = twist[0, rows_at]
        sine = twist[1, rows_at]
        out_real = real * cosine - imag * sine
        out_imag = real * sine + imag * cosine
        for part in range(tails):
            lanes = slice(part * breadth, (part + 1) * breadth)
            send_tail[at * tails + part, :fast_local] = out_real[:, lanes]
            send_tail[at * tails + part, fast_local:] = out_imag[:, lanes]

    def tail_copy(target, slot):
        return pltpu.make_async_remote_copy(
            src_ref=send_tail.at[target],
            dst_ref=recv_tail.at[slot],
            send_sem=tail_send.at[target],
            recv_sem=tail_recv.at[slot],
            device_id=place(target),
            device_id_type=MESH,
        )

    for step in range(1, members):
        tail_copy(lax.rem(me + step, members), me).start()
    recv_tail[me] = send_tail[me]
    for step in range(1, members):
        source = lax.rem(me + step, members)
        tail_copy(source, source).wait_recv()
    flat = recv_tail[...].reshape(members * 2 * fast_local, breadth)
    result = dot3(split(jnp.transpose(flat)), (final[0], final[1]))
    out_ref[0] = result[:, : rows * fast_len]
    out_ref[1] = result[:, rows * fast_len :]

    for step in range(1, members):
        target = lax.rem(me + step, members)
        tail_copy(target, me).wait_send()
    for step in range(1, groups):
        block_copy(lax.rem(group + step, groups)).wait_send()
    for chunk in range(CHUNKS):
        for slot in range(rows):

            @pl.when((slot <= row) & (row < rows - 1))
            def _():
                hop(x_ref, slot, chunk, 0, row + 1).wait_send()

            @pl.when((slot >= row) & (row > 0))
            def _():
                hop(x_ref, slot, chunk, 1, row - 1).wait_send()


def fused_on_device(sizes, trace):
    side, fast_len, fast_local, rows, groups, _ = sizes
    local_cols = trace.shape[0]
    low_len = side // fast_len
    half = low_len * fast_local
    wide = 2 * half
    members = rows * groups
    tables = [jnp.asarray(table) for table in fused_tables(sizes)]
    block = jnp.transpose(trace.reshape(local_cols, side, low_len, fast_local), (1, 0, 2, 3))
    block = block.reshape(side, wide)
    vmem = pltpu.VMEM
    bf16 = jnp.bfloat16
    f32 = jnp.float32
    dma = pltpu.SemaphoreType.DMA
    breadth = side * low_len // members
    return pl.pallas_call(
        partial(fused_kernel, sizes),
        out_shape=jax.ShapeDtypeStruct((2, breadth, rows * fast_len), f32),
        in_specs=[pl.BlockSpec(memory_space=vmem)]
        + [pl.BlockSpec(memory_space=pl.ANY)] * len(tables),
        out_specs=pl.BlockSpec(memory_space=vmem),
        scratch_shapes=[
            vmem((4, side, side), bf16),
            vmem((2, side, side), bf16),
            vmem((2, side, side), f32),
            vmem((2, half, side), f32),
            vmem((2, members * 2 * fast_local, 2 * rows * fast_len), bf16),
            vmem((rows, side, wide), f32),
            vmem((rows, side, wide), f32),
            vmem((8, wide), f32),
            vmem((2 * side, side), bf16),
            vmem((2 * side, side), bf16),
            vmem((2 * side, side), bf16),
            vmem((2 * side, side), bf16),
            vmem((groups, side + 8, wide), f32),
            vmem((groups, side + 8, wide), f32),
            vmem((members, 2 * fast_local, breadth), f32),
            vmem((members, 2 * fast_local, breadth), f32),
            vmem((2, side, side), f32),
            vmem((2, half, side), f32),
            dma((5,)),
            dma((rows, CHUNKS, 2)),
            dma((rows, CHUNKS)),
            dma((groups,)),
            dma((groups,)),
            dma((members,)),
            dma((members,)),
        ],
        compiler_params=pltpu.CompilerParams(
            collective_id=0, has_side_effects=True, vmem_limit_bytes=24 * 2**20
        ),
    )(block, *tables)


def fused_sizes(mesh, trace):
    shape = mesh.shape
    rows = shape["rows"]
    groups = shape["cols"] * shape["sub"]
    slow_len = trace.shape[1] // shape["groups"]
    fast_len = trace.shape[2]
    side = math.isqrt(slow_len * fast_len)
    fast_local = fast_len // rows
    local_cols = trace.shape[0] // groups
    low_len = side // fast_len
    fits = (
        side * side == slow_len * fast_len
        and low_len * fast_len == side
        and rows == 4
        and groups == rows
        and shape["cols"] == 2
        and shape["sub"] == 2
        and local_cols == 2
        and fast_local == 8
        and 2 * low_len * fast_local == 128
        and rows * groups == 2 * low_len
    )
    return (side, fast_len, fast_local, rows, groups, (shape["cols"], shape["sub"])) if fits else None


def solution(mesh):
    placed = (P(("cols", "sub"), "groups", "rows"),)

    def whole(trace):
        sizes = fused_sizes(mesh, trace)
        return jax.shard_map(
            on_device if sizes is None else partial(fused_on_device, sizes),
            mesh=mesh,
            in_specs=placed,
            out_specs=P("groups", ("rows", "cols", "sub"), None),
            check_vma=False,
        )(trace)

    return whole
```

```python
from functools import partial
import math

import jax
import jax.numpy as jnp
import numpy as np
from jax import lax
from jax.experimental import pallas as pl
from jax.experimental.pallas import tpu as pltpu
from jax.sharding import PartitionSpec as P


def dft_table(extent, orient):
    points = jnp.arange(extent, dtype=jnp.int32)
    product = points[:, None] * points[None, :] % extent
    angles = product.astype(jnp.float32) * (orient * 2.0 * math.pi / extent)
    return (jnp.cos(angles), jnp.sin(angles))


def complex_apply(table_real, table_imag, data_real, data_imag):
    matmul = partial(jnp.dot, precision=lax.Precision.HIGHEST, preferred_element_type=jnp.float32)
    out_real = matmul(table_real, data_real) - matmul(table_imag, data_imag)
    out_imag = matmul(table_real, data_imag) + matmul(table_imag, data_real)
    return (out_real, out_imag)


def rotate(data_real, data_imag, angles):
    cosine = jnp.cos(angles)
    sine = jnp.sin(angles)
    return (data_real * cosine - data_imag * sine, data_real * sine + data_imag * cosine)


def turn(index_product, modulus, orient):
    return (index_product % modulus).astype(jnp.float32) * (orient * 2.0 * math.pi / modulus)


def transform_lead(data_real, data_imag, orient):
    extent = data_real.shape[0]
    rest_shape = data_real.shape[1:]
    breadth = data_real.size // extent
    flat_real = data_real.reshape(extent, breadth)
    flat_imag = data_imag.reshape(extent, breadth)
    if extent <= 128:
        table_real, table_imag = dft_table(extent, orient)
        out_real, out_imag = complex_apply(table_real, table_imag, flat_real, flat_imag)
    else:
        outer_len = extent // 128
        first_real, first_imag = transform_lead(
            flat_real.reshape(outer_len, 128 * breadth),
            flat_imag.reshape(outer_len, 128 * breadth),
            orient,
        )
        first_real = first_real.reshape(outer_len, 128, breadth)
        first_imag = first_imag.reshape(outer_len, 128, breadth)
        outer_index = jnp.arange(outer_len, dtype=jnp.int32)[:, None]
        inner_index = jnp.arange(128, dtype=jnp.int32)[None, :]
        angles = turn(outer_index * inner_index, extent, orient)[:, :, None]
        first_real, first_imag = rotate(first_real, first_imag, angles)
        first_real = jnp.transpose(first_real, (1, 0, 2)).reshape(128, outer_len * breadth)
        first_imag = jnp.transpose(first_imag, (1, 0, 2)).reshape(128, outer_len * breadth)
        out_real, out_imag = transform_lead(first_real, first_imag, orient)
    return (out_real.reshape((extent,) + rest_shape), out_imag.reshape((extent,) + rest_shape))


def times(first, second):
    return (
        first[0] * second[0] - first[1] * second[1],
        first[0] * second[1] + first[1] * second[0],
    )


def plus(first, second):
    return (first[0] + second[0], first[1] + second[1])


def on_device(trace):
    local_cols = trace.shape[0]
    slow_len = trace.shape[1]
    fast_local = trace.shape[2]
    row_parts = lax.axis_size("rows")
    group_parts = lax.axis_size(("cols", "sub"))
    row_index = lax.axis_index("rows")
    group_index = lax.axis_index(("cols", "sub"))
    fast_len = fast_local * row_parts
    trace_len = slow_len * fast_len
    ext_len = 4 * trace_len
    ext_slow = 4 * fast_len
    slow_block = slow_len // row_parts
    ext_block = ext_slow // row_parts
    point_block = ext_block // group_parts
    coeff_block = slow_block // group_parts
    real_part = jnp.transpose(trace, (1, 0, 2))
    imag_part = jnp.zeros_like(real_part)
    real_part, imag_part = transform_lead(real_part, imag_part, 1.0)
    lead_index = jnp.arange(slow_len, dtype=jnp.int32)[:, None, None]
    fast_index = (row_index * fast_local + jnp.arange(fast_local, dtype=jnp.int32))[None, None, :]
    real_part, imag_part = rotate(
        real_part, imag_part, turn(lead_index * fast_index, trace_len, 1.0)
    )
    moved = lax.all_to_all(
        jnp.stack([real_part, imag_part]), "rows", split_axis=1, concat_axis=3, tiled=True
    )
    moved = jnp.transpose(moved, (0, 3, 2, 1))
    real_part, imag_part = transform_lead(moved[0], moved[1], 1.0)
    slow_index = (row_index * slow_block + jnp.arange(slow_block, dtype=jnp.int32))[None, None, :]
    coeff_index = jnp.arange(fast_len, dtype=jnp.int32)[:, None, None] * slow_len + slow_index
    shift_angle = coeff_index.astype(jnp.float32) * (math.pi / (4.0 * trace_len))
    real_part, imag_part = rotate(real_part / trace_len, imag_part / trace_len, shift_angle)
    padding = jnp.zeros((ext_slow - fast_len, local_cols, slow_index.shape[2]), jnp.float32)
    real_part = jnp.concatenate([real_part, padding], 0)
    imag_part = jnp.concatenate([imag_part, padding], 0)
    real_part, imag_part = transform_lead(real_part, imag_part, -1.0)
    ext_index = jnp.arange(ext_slow, dtype=jnp.int32)[:, None, None]
    real_part, imag_part = rotate(real_part, imag_part, turn(ext_index * slow_index, ext_len, -1.0))
    stacked = jnp.stack([real_part, imag_part])
    moved = lax.all_to_all(stacked, "rows", split_axis=1, concat_axis=3, tiled=True)
    moved = jnp.transpose(moved, (0, 3, 2, 1))
    real_part, imag_part = transform_lead(moved[0], moved[1], -1.0)
    joined = lax.all_to_all(
        jnp.stack([real_part, imag_part]), ("cols", "sub"), split_axis=3, concat_axis=2, tiled=True
    )
    real_part = joined[0]
    imag_part = joined[1]

    def column(number):
        return (real_part[:, number], imag_part[:, number])

    wire_a = column(0)
    wire_b = column(1)
    wire_c = column(2)
    gate = times(times(times(column(3), wire_a), wire_b), wire_c)
    gate = plus(gate, times(column(4), wire_a))
    gate = plus(gate, times(column(5), wire_b))
    gate = plus(gate, times(column(6), wire_c))
    gate = plus(gate, column(7))
    point_index = (
        row_index * ext_block + group_index * point_block + jnp.arange(point_block, dtype=jnp.int32)
    )
    quarter = (point_index % 4).astype(jnp.float32)
    vanish_angle = math.pi / 4.0 - math.pi / 2.0 * quarter
    vanish_real = (jnp.cos(vanish_angle) - 1.0)[None, :]
    vanish_imag = jnp.sin(vanish_angle)[None, :]
    magnitude = vanish_real * vanish_real + vanish_imag * vanish_imag
    ratio_real = (gate[0] * vanish_real + gate[1] * vanish_imag) / magnitude
    ratio_imag = (gate[1] * vanish_real - gate[0] * vanish_imag) / magnitude
    real_part, imag_part = transform_lead(ratio_real, ratio_imag, 1.0)
    freq_index = jnp.arange(slow_len, dtype=jnp.int32)[:, None]
    real_part, imag_part = rotate(
        real_part, imag_part, turn(freq_index * point_index[None, :], ext_len, 1.0)
    )
    moved = lax.all_to_all(
        lax.all_to_all(
            jnp.stack([real_part, imag_part]), "rows", split_axis=1, concat_axis=2, tiled=True
        ),
        ("cols", "sub"),
        split_axis=1,
        concat_axis=2,
        tiled=True,
    )
    moved = moved.reshape(2, coeff_block, group_parts, row_parts, point_block)
    moved = jnp.transpose(moved, (0, 3, 2, 4, 1)).reshape(2, ext_slow, coeff_block)
    real_part, imag_part = transform_lead(moved[0], moved[1], 1.0)
    low_index = (
        row_index * slow_block
        + group_index * coeff_block
        + jnp.arange(coeff_block, dtype=jnp.int32)
    )[None, :]
    final_index = jnp.arange(ext_slow, dtype=jnp.int32)[:, None] * slow_len + low_index
    final_angle = final_index.astype(jnp.float32) * (-math.pi / (4.0 * trace_len))
    real_part, imag_part = rotate(real_part, imag_part, final_angle)
    result = jnp.stack([real_part, imag_part]) * (1.0 / math.sqrt(ext_len))
    return jnp.transpose(result, (0, 2, 1))


MESH = pl.DeviceIdType.MESH
CHUNKS = 4


def halves(table):
    high = table.astype(jnp.bfloat16)
    low = (table - high.astype(np.float64)).astype(jnp.bfloat16)
    return high, low


def fused_tables(sizes):
    side, fast_len, fast_local, rows, groups, blocks = sizes
    points = side * side
    ext = rows * points
    low_len = side // fast_len
    slow_len = side * low_len
    index = np.arange(side)
    angles = 2.0 * np.pi * (index[:, None] * index[None, :] % side) / side
    dft = np.stack(halves(np.cos(angles)) + halves(np.sin(angles)))
    row_at, low_at, fast_at = (
        grid.reshape(-1)
        for grid in np.meshgrid(
            np.arange(rows), np.arange(low_len), np.arange(fast_local), indexing="ij"
        )
    )
    inner = fast_local * row_at + fast_at
    centred = low_at[:, None] + low_len * index[None, :] - slow_len // 2
    theta = 2.0 * np.pi * inner[:, None] * centred / points
    base = np.stack([np.cos(theta), np.sin(theta)]).astype(np.float32)
    shifts = 0.5 / rows - np.arange(rows) / rows
    same = low_at[:, None] == low_at[None, :]
    sign = 1.0 - 2.0 * (inner[:, None] % 2)
    kernels = []
    for shift in shifts:
        gap = inner[None, :] - inner[:, None] + shift
        weight = sign / points * np.sin(np.pi * shift) / np.sin(np.pi * gap / fast_len)
        kernels.append(np.stack(halves(np.where(same, weight, 0.0))))
    kernels = np.stack(kernels)
    low_index = np.repeat(np.arange(low_len), fast_local)
    spin = 2.0 * np.pi * low_index[:, None] * index[None, :] / slow_len
    spin = np.stack([np.cos(spin), np.sin(spin)]).astype(np.float32)
    source_row, source_group, fast_at = np.meshgrid(
        np.arange(rows), np.arange(groups), np.arange(fast_local), indexing="ij"
    )
    low_digit = rows * (fast_local * source_group + fast_at) + source_row
    vanish = np.exp(1j * (np.pi / rows - 2.0 * np.pi / rows * source_row)) - 1.0
    finals = np.arange(rows * fast_len)
    turns = np.exp(
        2j * np.pi * low_digit[..., None] * finals / (rows * fast_len)
        - 1j * np.pi * slow_len * finals / ext
    ) / (vanish[..., None] * math.sqrt(ext))
    real_rows = np.concatenate([turns.real, turns.imag], -1)
    imag_rows = np.concatenate([-turns.imag, turns.real], -1)
    final = np.stack([real_rows, imag_rows], 2).reshape(-1, 2 * rows * fast_len)
    final = np.stack(halves(final))
    return dft, kernels, base, spin, final


def split(value):
    high = value.astype(jnp.bfloat16)
    return high, (value - high.astype(jnp.float32)).astype(jnp.bfloat16)


def dot3(left, right):
    mul = partial(jnp.dot, preferred_element_type=jnp.float32)
    return mul(left[0], right[0]) + (mul(left[0], right[1]) + mul(left[1], right[0]))


def short_transform(values, orient):
    count = len(values)
    if count == 1:
        return values
    even = short_transform(values[0::2], orient)
    odd = short_transform(values[1::2], orient)
    first, second = [], []
    for at in range(count // 2):
        cosine = math.cos(2.0 * math.pi * at / count)
        sine = orient * math.sin(2.0 * math.pi * at / count)
        real, imag = odd[at]
        if at == 0:
            spun = (real, imag)
        elif 4 * at == count:
            spun = (-orient * imag, orient * real)
        else:
            spun = (real * cosine - imag * sine, real * sine + imag * cosine)
        first.append(plus(even[at], spun))
        second.append((even[at][0] - spun[0], even[at][1] - spun[1]))
    return first + second


def fused_kernel(
    sizes,
    x_ref,
    dft_hbm,
    kern_hbm,
    base_hbm,
    spin_hbm,
    final_hbm,
    out_ref,
    dft,
    kern,
    base,
    spin,
    final,
    gathered,
    total,
    data_high,
    data_low,
    wide,
    send_block,
    recv_block,
    send_tail,
    recv_tail,
    post,
    twist,
    table_sem,
    gather_send,
    gather_recv,
    block_send,
    block_recv,
    tail_send,
    tail_recv,
):
    side, fast_len, fast_local, rows, groups, (cols, subs) = sizes
    points = side * side
    ext = rows * points
    low_len = side // fast_len
    half = low_len * fast_local
    piece = side * low_len // CHUNKS
    members = rows * groups
    row = lax.axis_index("rows")
    col = lax.axis_index("cols")
    sub = lax.axis_index("sub")
    group = col * subs + sub
    me = row * groups + group

    def place(member):
        inside = lax.rem(member, groups)
        return {
            "rows": lax.div(member, groups),
            "cols": lax.div(inside, subs),
            "sub": lax.rem(inside, subs),
        }

    barrier = pltpu.get_barrier_semaphore()
    for step in range(1, groups):
        other = lax.rem(group + step, groups)
        pl.semaphore_signal(
            barrier,
            inc=1,
            device_id={"cols": lax.div(other, subs), "sub": lax.rem(other, subs)},
            device_id_type=MESH,
        )

    @pl.when(row > 0)
    def _():
        pl.semaphore_signal(barrier, inc=1, device_id={"rows": row - 1}, device_id_type=MESH)

    @pl.when(row < rows - 1)
    def _():
        pl.semaphore_signal(barrier, inc=1, device_id={"rows": row + 1}, device_id_type=MESH)

    loads = [
        pltpu.make_async_copy(dft_hbm, dft, table_sem.at[0]),
        pltpu.make_async_copy(base_hbm, base, table_sem.at[1]),
        pltpu.make_async_copy(kern_hbm.at[row], kern, table_sem.at[2]),
        pltpu.make_async_copy(spin_hbm, spin, table_sem.at[3]),
        pltpu.make_async_copy(final_hbm, final, table_sem.at[4]),
    ]
    for load in loads:
        load.start()
    pl.semaphore_wait(
        barrier,
        groups - 1 + (row > 0).astype(jnp.int32) + (row < rows - 1).astype(jnp.int32),
    )

    def hop(source, slot, chunk, way, target):
        span = pl.ds(chunk * piece, piece)
        return pltpu.make_async_remote_copy(
            src_ref=source.at[:, :, span],
            dst_ref=gathered.at[slot, :, :, span],
            send_sem=gather_send.at[slot, chunk, way],
            recv_sem=gather_recv.at[slot, chunk],
            device_id={"rows": target},
            device_id_type=MESH,
        )

    for chunk in range(CHUNKS):

        @pl.when(row < rows - 1)
        def _():
            hop(x_ref, row, chunk, 0, row + 1).start()

        @pl.when(row > 0)
        def _():
            hop(x_ref, row, chunk, 1, row - 1).start()

    own = pltpu.make_async_copy(x_ref, gathered.at[row], table_sem.at[5])
    own.start()

    def stacked(values):
        return jnp.concatenate([value for value in values], 0)

    def slices(real, imag):
        return [
            (real[at * fast_local : (at + 1) * fast_local], imag[at * fast_local : (at + 1) * fast_local])
            for at in range(low_len)
        ]

    def lane_transform(real, imag, orient):
        count = real.shape[0]
        data = split(jnp.concatenate([real, imag], 0))
        cosines = dot3(data, (dft[0], dft[1]))
        sines = dot3(data, (dft[2], dft[3]))
        return (
            cosines[:count] - orient * sines[count:],
            cosines[count:] + orient * sines[:count],
        )

    def first_stage(slot):
        values = [
            (
                gathered[slot, 0, :, at * side : (at + 1) * side],
                gathered[slot, 1, :, at * side : (at + 1) * side],
            )
            for at in range(low_len)
        ]
        for at in range(2):
            sums = values[0][at]
            for value in values[1:]:
                sums = sums + value[at]
            total[at] += sums
        values = short_transform(values, 1.0)
        real = stacked([value[0] for value in values])
        imag = stacked([value[1] for value in values])
        real, imag = times((real, imag), (spin[0], spin[1]))
        real, imag = lane_transform(real, imag, 1.0)
        span = pl.ds(pl.multiple_of(slot * half, half), half)
        real, imag = times((real, imag), (base[0, span], base[1, span]))
        high, low = split(real)
        data_high[span, :side] = high
        data_low[span, :side] = low
        high, low = split(imag)
        data_high[span, side:] = high
        data_low[span, side:] = low

    shift = 0.5 / rows - row.astype(jnp.float32) / rows
    at_row = lax.broadcasted_iota(jnp.int32, (half, side), 0)
    at_lane = lax.broadcasted_iota(jnp.int32, (half, side), 1)
    low_freq = at_row // fast_local + low_len * at_lane
    digit = rows * (fast_local * group + at_row % fast_local) + row
    total[...] = jnp.zeros_like(total)
    own.wait()
    loads[0].wait()
    loads[1].wait()
    loads[3].wait()
    first_stage(row)
    centred = (low_freq - side * low_len // 2).astype(jnp.float32)
    angle = centred * (shift * (2.0 * math.pi / points))
    turn_cos = jnp.cos(angle)
    turn_sin = jnp.sin(angle)
    for at in range(rows):
        span = slice(at * half, (at + 1) * half)
        post[0, span] = base[0, span] * turn_cos + base[1, span] * turn_sin
        post[1, span] = base[0, span] * turn_sin - base[1, span] * turn_cos
    tail_angle = ((low_freq * (2 * digit - 1)) % (2 * ext)).astype(jnp.float32) * (math.pi / ext)
    twist[0] = jnp.cos(tail_angle)
    twist[1] = jnp.sin(tail_angle)

    @pl.loop(0, rows - 1)
    def _(step):
        inner = jnp.where(
            step == 0, row - 1, jnp.where(step == 1, row + 1, 2 * rows - 2 - 3 * row)
        )
        slot = jnp.where(
            row == 0, step + 1, jnp.where(row == rows - 1, rows - 2 - step, inner)
        )
        for chunk in range(CHUNKS):
            hop(x_ref, slot, chunk, 0, row).wait_recv()

            @pl.when((slot < row) & (row < rows - 1))
            def _():
                hop(gathered.at[slot], slot, chunk, 0, row + 1).start()

            @pl.when((slot > row) & (row > 0))
            def _():
                hop(gathered.at[slot], slot, chunk, 1, row - 1).start()

        first_stage(slot)

    mean_a = jnp.sum(jnp.sum(total[0], 0, keepdims=True), 1, keepdims=True) * (1.0 / points)
    mean_b = jnp.sum(jnp.sum(total[1], 0, keepdims=True), 1, keepdims=True) * (1.0 / points)
    loads[2].wait()
    moved = dot3((kern[0], kern[1]), (data_high[...], data_low[...]))
    real, imag = times((moved[:, :side], moved[:, side:]), (post[0], post[1]))
    half_turn = jnp.zeros((1, 1), jnp.float32) + shift * math.pi
    half_cos = jnp.cos(half_turn)
    half_sin = jnp.sin(half_turn)
    row_at = lax.broadcasted_iota(jnp.int32, (rows * half, side), 0)
    lane_at = lax.broadcasted_iota(jnp.int32, (rows * half, side), 1)
    constant = (lane_at == 0) & (row_at % half < fast_local)
    parity = jnp.where(constant, (1 - 2 * (row_at % 2)).astype(jnp.float32), 0.0)
    wide[0] = real - parity * (mean_a * half_cos + mean_b * half_sin)
    wide[1] = imag - parity * (mean_b * half_cos - mean_a * half_sin)
    side_at = lax.broadcasted_iota(jnp.int32, (8, side), 1)
    means = jnp.where(side_at < side // 2, mean_a, mean_b)

    def block_copy(target):
        return pltpu.make_async_remote_copy(
            src_ref=send_block.at[target],
            dst_ref=recv_block.at[group],
            send_sem=block_send.at[target],
            recv_sem=block_recv.at[group],
            device_id={"cols": lax.div(target, subs), "sub": lax.rem(target, subs)},
            device_id_type=MESH,
        )

    def block_arrival(source):
        return pltpu.make_async_remote_copy(
            src_ref=send_block.at[source],
            dst_ref=recv_block.at[source],
            send_sem=block_send.at[source],
            recv_sem=block_recv.at[source],
            device_id={"cols": lax.div(source, subs), "sub": lax.rem(source, subs)},
            device_id_type=MESH,
        )

    @pl.loop(0, cols)
    def _(step):
        tile = lax.rem(col + 1 + step, cols)
        span = pl.ds(pl.multiple_of(tile * subs * half, subs * half), subs * half)
        real, imag = lane_transform(wide[0, span], wide[1, span], -1.0)
        for at in range(subs):
            target = tile * subs + at
            values = times(
                (real[at * half : (at + 1) * half], imag[at * half : (at + 1) * half]),
                (spin[0], -spin[1]),
            )
            values = short_transform(slices(*values), -1.0)
            for low in range(low_len):
                rows_at = slice(low * fast_local, (low + 1) * fast_local)
                send_block[target, rows_at] = values[low][0]
                send_block[target, half + low * fast_local : half + (low + 1) * fast_local] = (
                    values[low][1]
                )
            send_block[target, 2 * half :] = means

            @pl.when(target != group)
            def _():
                block_copy(target).start()

    recv_block[group] = send_block[group]
    for step in range(1, groups):
        block_arrival(lax.rem(group + step, groups)).wait_recv()

    flip = (1 - 2 * (at_row % 2)).astype(jnp.float32)
    part_cos = flip * half_cos
    part_sin = flip * half_sin

    def value(number):
        block, at = divmod(number, 2)
        data = recv_block[block, at * half : (at + 1) * half]
        lane_from = at * (side // 2)
        mean = recv_block[block, 2 * half : 2 * half + 1, lane_from : lane_from + 1]
        return (mean + part_cos * data, part_sin * data)

    wire_a = value(0)
    wire_b = value(1)
    wire_c = value(2)
    gate = times(times(times(value(3), wire_a), wire_b), wire_c)
    gate = plus(gate, times(value(4), wire_a))
    gate = plus(gate, times(value(5), wire_b))
    gate = plus(gate, times(value(6), wire_c))
    gate = plus(gate, value(7))
    values = short_transform(slices(*gate), 1.0)
    real = stacked([value[0] for value in values])
    imag = stacked([value[1] for value in values])
    real, imag = times((real, imag), (spin[0], spin[1]))
    real, imag = lane_transform(real, imag, 1.0)
    real, imag = times((real, imag), (twist[0], twist[1]))
    loads[4].wait()

    breadth = side * low_len // members
    lane_piece = side // members
    tile_lanes = low_len * lane_piece
    lanes = lax.broadcasted_iota(jnp.int32, (2 * fast_local, tile_lanes), 1)
    for tile in range(side // tile_lanes):
        span = slice(tile * tile_lanes, (tile + 1) * tile_lanes)
        pieces = [
            jnp.concatenate(
                [
                    real[at * fast_local : (at + 1) * fast_local, span],
                    imag[at * fast_local : (at + 1) * fast_local, span],
                ],
                0,
            )
            for at in range(low_len)
        ]
        bit = low_len // 2
        while bit:
            keep = (lanes // (lane_piece * bit)) % 2 == 0
            for at in range(low_len):
                if at & bit == 0:
                    first, second = pieces[at], pieces[at + bit]
                    pieces[at] = jnp.where(keep, first, pltpu.roll(second, lane_piece * bit, 1))
                    pieces[at + bit] = jnp.where(
                        keep, pltpu.roll(first, tile_lanes - lane_piece * bit, 1), second
                    )
            bit //= 2
        for at in range(low_len):
            send_tail[tile * low_len + at] = pieces[at]

    def tail_copy(target, slot):
        return pltpu.make_async_remote_copy(
            src_ref=send_tail.at[target],
            dst_ref=recv_tail.at[slot],
            send_sem=tail_send.at[target],
            recv_sem=tail_recv.at[slot],
            device_id=place(target),
            device_id_type=MESH,
        )

    for step in range(1, members):
        tail_copy(lax.rem(me + step, members), me).start()
    recv_tail[me] = send_tail[me]
    for step in range(1, members):
        source = lax.rem(me + step, members)
        tail_copy(source, source).wait_recv()
    flat = recv_tail[...].reshape(members * 2 * fast_local, breadth)
    result = dot3(split(jnp.transpose(flat)), (final[0], final[1]))
    for at in range(low_len):
        picked = result[at * lane_piece : (at + 1) * lane_piece]
        rows_at = pl.ds(at, lane_piece, stride=low_len)
        out_ref[0, rows_at] = picked[:, : rows * fast_len]
        out_ref[1, rows_at] = picked[:, rows * fast_len :]

    for step in range(1, members):
        target = lax.rem(me + step, members)
        tail_copy(target, me).wait_send()
    for step in range(1, groups):
        block_copy(lax.rem(group + step, groups)).wait_send()
    for chunk in range(CHUNKS):
        for slot in range(rows):

            @pl.when((slot <= row) & (row < rows - 1))
            def _():
                hop(x_ref, slot, chunk, 0, row + 1).wait_send()

            @pl.when((slot >= row) & (row > 0))
            def _():
                hop(x_ref, slot, chunk, 1, row - 1).wait_send()


def fused_on_device(sizes, trace):
    side, fast_len, fast_local, rows, groups, _ = sizes
    low_len = side // fast_len
    half = low_len * fast_local
    members = rows * groups
    tables = [jnp.asarray(table) for table in fused_tables(sizes)]
    block = jnp.transpose(trace, (0, 2, 1))
    vmem = pltpu.VMEM
    bf16 = jnp.bfloat16
    f32 = jnp.float32
    dma = pltpu.SemaphoreType.DMA
    breadth = side * low_len // members
    return pl.pallas_call(
        partial(fused_kernel, sizes),
        out_shape=jax.ShapeDtypeStruct((2, breadth, rows * fast_len), f32),
        in_specs=[pl.BlockSpec(memory_space=pltpu.HBM)] * (1 + len(tables)),
        out_specs=pl.BlockSpec(memory_space=vmem),
        scratch_shapes=[
            vmem((4, side, side), bf16),
            vmem((2, side, side), bf16),
            vmem((2, side, side), f32),
            vmem((2, half, side), f32),
            vmem((2, members * 2 * fast_local, 2 * rows * fast_len), bf16),
            vmem((rows,) + block.shape, f32),
            vmem((2, fast_local, side), f32),
            vmem((side, 2 * side), bf16),
            vmem((side, 2 * side), bf16),
            vmem((2, side, side), f32),
            vmem((groups, 2 * half + 8, side), f32),
            vmem((groups, 2 * half + 8, side), f32),
            vmem((members, 2 * fast_local, breadth), f32),
            vmem((members, 2 * fast_local, breadth), f32),
            vmem((2, side, side), f32),
            vmem((2, half, side), f32),
            dma((6,)),
            dma((rows, CHUNKS, 2)),
            dma((rows, CHUNKS)),
            dma((groups,)),
            dma((groups,)),
            dma((members,)),
            dma((members,)),
        ],
        compiler_params=pltpu.CompilerParams(
            collective_id=0, has_side_effects=True, vmem_limit_bytes=67043328 - 288 * 1024
        ),
    )(block, *tables)


def fused_sizes(mesh, trace):
    shape = mesh.shape
    rows = shape["rows"]
    groups = shape["cols"] * shape["sub"]
    slow_len = trace.shape[1] // shape["groups"]
    fast_len = trace.shape[2]
    side = math.isqrt(slow_len * fast_len)
    fast_local = fast_len // rows
    local_cols = trace.shape[0] // groups
    low_len = side // fast_len
    fits = (
        side * side == slow_len * fast_len
        and low_len * fast_len == side
        and rows == 4
        and groups == rows
        and shape["cols"] == 2
        and shape["sub"] == 2
        and local_cols == 2
        and fast_local == 8
        and 2 * low_len * fast_local == 128
        and rows * groups == 2 * low_len
    )
    return (side, fast_len, fast_local, rows, groups, (shape["cols"], shape["sub"])) if fits else None


def solution(mesh):
    placed = (P(("cols", "sub"), "groups", "rows"),)

    def whole(trace):
        sizes = fused_sizes(mesh, trace)
        return jax.shard_map(
            on_device if sizes is None else partial(fused_on_device, sizes),
            mesh=mesh,
            in_specs=placed,
            out_specs=P("groups", ("rows", "cols", "sub"), None),
            check_vma=False,
        )(trace)

    return whole
```

```python
from functools import partial
import math

import jax
import jax.numpy as jnp
import numpy as np
from jax import lax
from jax.experimental import pallas as pl
from jax.experimental.pallas import tpu as pltpu
from jax.sharding import PartitionSpec as P


def dft_table(extent, orient):
    points = jnp.arange(extent, dtype=jnp.int32)
    product = points[:, None] * points[None, :] % extent
    angles = product.astype(jnp.float32) * (orient * 2.0 * math.pi / extent)
    return (jnp.cos(angles), jnp.sin(angles))


def complex_apply(table_real, table_imag, data_real, data_imag):
    matmul = partial(jnp.dot, precision=lax.Precision.HIGHEST, preferred_element_type=jnp.float32)
    out_real = matmul(table_real, data_real) - matmul(table_imag, data_imag)
    out_imag = matmul(table_real, data_imag) + matmul(table_imag, data_real)
    return (out_real, out_imag)


def rotate(data_real, data_imag, angles):
    cosine = jnp.cos(angles)
    sine = jnp.sin(angles)
    return (data_real * cosine - data_imag * sine, data_real * sine + data_imag * cosine)


def turn(index_product, modulus, orient):
    return (index_product % modulus).astype(jnp.float32) * (orient * 2.0 * math.pi / modulus)


def transform_lead(data_real, data_imag, orient):
    extent = data_real.shape[0]
    rest_shape = data_real.shape[1:]
    breadth = data_real.size // extent
    flat_real = data_real.reshape(extent, breadth)
    flat_imag = data_imag.reshape(extent, breadth)
    if extent <= 128:
        table_real, table_imag = dft_table(extent, orient)
        out_real, out_imag = complex_apply(table_real, table_imag, flat_real, flat_imag)
    else:
        outer_len = extent // 128
        first_real, first_imag = transform_lead(
            flat_real.reshape(outer_len, 128 * breadth),
            flat_imag.reshape(outer_len, 128 * breadth),
            orient,
        )
        first_real = first_real.reshape(outer_len, 128, breadth)
        first_imag = first_imag.reshape(outer_len, 128, breadth)
        outer_index = jnp.arange(outer_len, dtype=jnp.int32)[:, None]
        inner_index = jnp.arange(128, dtype=jnp.int32)[None, :]
        angles = turn(outer_index * inner_index, extent, orient)[:, :, None]
        first_real, first_imag = rotate(first_real, first_imag, angles)
        first_real = jnp.transpose(first_real, (1, 0, 2)).reshape(128, outer_len * breadth)
        first_imag = jnp.transpose(first_imag, (1, 0, 2)).reshape(128, outer_len * breadth)
        out_real, out_imag = transform_lead(first_real, first_imag, orient)
    return (out_real.reshape((extent,) + rest_shape), out_imag.reshape((extent,) + rest_shape))


def times(first, second):
    return (
        first[0] * second[0] - first[1] * second[1],
        first[0] * second[1] + first[1] * second[0],
    )


def plus(first, second):
    return (first[0] + second[0], first[1] + second[1])


def on_device(trace):
    local_cols = trace.shape[0]
    slow_len = trace.shape[1]
    fast_local = trace.shape[2]
    row_parts = lax.axis_size("rows")
    group_parts = lax.axis_size(("cols", "sub"))
    row_index = lax.axis_index("rows")
    group_index = lax.axis_index(("cols", "sub"))
    fast_len = fast_local * row_parts
    trace_len = slow_len * fast_len
    ext_len = 4 * trace_len
    ext_slow = 4 * fast_len
    slow_block = slow_len // row_parts
    ext_block = ext_slow // row_parts
    point_block = ext_block // group_parts
    coeff_block = slow_block // group_parts
    real_part = jnp.transpose(trace, (1, 0, 2))
    imag_part = jnp.zeros_like(real_part)
    real_part, imag_part = transform_lead(real_part, imag_part, 1.0)
    lead_index = jnp.arange(slow_len, dtype=jnp.int32)[:, None, None]
    fast_index = (row_index * fast_local + jnp.arange(fast_local, dtype=jnp.int32))[None, None, :]
    real_part, imag_part = rotate(
        real_part, imag_part, turn(lead_index * fast_index, trace_len, 1.0)
    )
    moved = lax.all_to_all(
        jnp.stack([real_part, imag_part]), "rows", split_axis=1, concat_axis=3, tiled=True
    )
    moved = jnp.transpose(moved, (0, 3, 2, 1))
    real_part, imag_part = transform_lead(moved[0], moved[1], 1.0)
    slow_index = (row_index * slow_block + jnp.arange(slow_block, dtype=jnp.int32))[None, None, :]
    coeff_index = jnp.arange(fast_len, dtype=jnp.int32)[:, None, None] * slow_len + slow_index
    shift_angle = coeff_index.astype(jnp.float32) * (math.pi / (4.0 * trace_len))
    real_part, imag_part = rotate(real_part / trace_len, imag_part / trace_len, shift_angle)
    padding = jnp.zeros((ext_slow - fast_len, local_cols, slow_index.shape[2]), jnp.float32)
    real_part = jnp.concatenate([real_part, padding], 0)
    imag_part = jnp.concatenate([imag_part, padding], 0)
    real_part, imag_part = transform_lead(real_part, imag_part, -1.0)
    ext_index = jnp.arange(ext_slow, dtype=jnp.int32)[:, None, None]
    real_part, imag_part = rotate(real_part, imag_part, turn(ext_index * slow_index, ext_len, -1.0))
    stacked = jnp.stack([real_part, imag_part])
    moved = lax.all_to_all(stacked, "rows", split_axis=1, concat_axis=3, tiled=True)
    moved = jnp.transpose(moved, (0, 3, 2, 1))
    real_part, imag_part = transform_lead(moved[0], moved[1], -1.0)
    joined = lax.all_to_all(
        jnp.stack([real_part, imag_part]), ("cols", "sub"), split_axis=3, concat_axis=2, tiled=True
    )
    real_part = joined[0]
    imag_part = joined[1]

    def column(number):
        return (real_part[:, number], imag_part[:, number])

    wire_a = column(0)
    wire_b = column(1)
    wire_c = column(2)
    gate = times(times(times(column(3), wire_a), wire_b), wire_c)
    gate = plus(gate, times(column(4), wire_a))
    gate = plus(gate, times(column(5), wire_b))
    gate = plus(gate, times(column(6), wire_c))
    gate = plus(gate, column(7))
    point_index = (
        row_index * ext_block + group_index * point_block + jnp.arange(point_block, dtype=jnp.int32)
    )
    quarter = (point_index % 4).astype(jnp.float32)
    vanish_angle = math.pi / 4.0 - math.pi / 2.0 * quarter
    vanish_real = (jnp.cos(vanish_angle) - 1.0)[None, :]
    vanish_imag = jnp.sin(vanish_angle)[None, :]
    magnitude = vanish_real * vanish_real + vanish_imag * vanish_imag
    ratio_real = (gate[0] * vanish_real + gate[1] * vanish_imag) / magnitude
    ratio_imag = (gate[1] * vanish_real - gate[0] * vanish_imag) / magnitude
    real_part, imag_part = transform_lead(ratio_real, ratio_imag, 1.0)
    freq_index = jnp.arange(slow_len, dtype=jnp.int32)[:, None]
    real_part, imag_part = rotate(
        real_part, imag_part, turn(freq_index * point_index[None, :], ext_len, 1.0)
    )
    moved = lax.all_to_all(
        lax.all_to_all(
            jnp.stack([real_part, imag_part]), "rows", split_axis=1, concat_axis=2, tiled=True
        ),
        ("cols", "sub"),
        split_axis=1,
        concat_axis=2,
        tiled=True,
    )
    moved = moved.reshape(2, coeff_block, group_parts, row_parts, point_block)
    moved = jnp.transpose(moved, (0, 3, 2, 4, 1)).reshape(2, ext_slow, coeff_block)
    real_part, imag_part = transform_lead(moved[0], moved[1], 1.0)
    low_index = (
        row_index * slow_block
        + group_index * coeff_block
        + jnp.arange(coeff_block, dtype=jnp.int32)
    )[None, :]
    final_index = jnp.arange(ext_slow, dtype=jnp.int32)[:, None] * slow_len + low_index
    final_angle = final_index.astype(jnp.float32) * (-math.pi / (4.0 * trace_len))
    real_part, imag_part = rotate(real_part, imag_part, final_angle)
    result = jnp.stack([real_part, imag_part]) * (1.0 / math.sqrt(ext_len))
    return jnp.transpose(result, (0, 2, 1))


MESH = pl.DeviceIdType.MESH
CHUNKS = 4


def halves(table):
    high = table.astype(jnp.bfloat16)
    low = (table - high.astype(np.float64)).astype(jnp.bfloat16)
    return high, low


def fused_tables(sizes):
    side, fast_len, fast_local, rows, groups, blocks = sizes
    points = side * side
    ext = rows * points
    low_len = side // fast_len
    slow_len = side * low_len
    index = np.arange(side)
    angles = 2.0 * np.pi * (index[:, None] * index[None, :] % side) / side
    dft = np.stack(halves(np.cos(angles)) + halves(np.sin(angles)))
    row_at, low_at, fast_at = (
        grid.reshape(-1)
        for grid in np.meshgrid(
            np.arange(rows), np.arange(low_len), np.arange(fast_local), indexing="ij"
        )
    )
    inner = fast_local * row_at + fast_at
    centred = low_at[:, None] + low_len * index[None, :] - slow_len // 2
    theta = 2.0 * np.pi * inner[:, None] * centred / points
    base = np.stack([np.cos(theta), np.sin(theta)]).astype(np.float32)
    shifts = 0.5 / rows - np.arange(rows) / rows
    same = low_at[:, None] == low_at[None, :]
    sign = 1.0 - 2.0 * (inner[:, None] % 2)
    kernels = []
    for shift in shifts:
        gap = inner[None, :] - inner[:, None] + shift
        weight = sign / points * np.sin(np.pi * shift) / np.sin(np.pi * gap / fast_len)
        kernels.append(np.stack(halves(np.where(same, weight, 0.0))))
    kernels = np.stack(kernels)
    low_index = np.repeat(np.arange(low_len), fast_local)
    spin = 2.0 * np.pi * low_index[:, None] * index[None, :] / slow_len
    spin = np.stack([np.cos(spin), np.sin(spin)]).astype(np.float32)
    source_row, source_group, fast_at = np.meshgrid(
        np.arange(rows), np.arange(groups), np.arange(fast_local), indexing="ij"
    )
    low_digit = rows * (fast_local * source_group + fast_at) + source_row
    vanish = np.exp(1j * (np.pi / rows - 2.0 * np.pi / rows * source_row)) - 1.0
    finals = np.arange(rows * fast_len)
    turns = np.exp(
        2j * np.pi * low_digit[..., None] * finals / (rows * fast_len)
        - 1j * np.pi * slow_len * finals / ext
    ) / (vanish[..., None] * math.sqrt(ext))
    real_rows = np.concatenate([turns.real, turns.imag], -1)
    imag_rows = np.concatenate([-turns.imag, turns.real], -1)
    final = np.stack([real_rows, imag_rows], 2).reshape(-1, 2 * rows * fast_len)
    final = np.stack(halves(final))
    return dft, kernels, base, spin, final


def split(value):
    high = value.astype(jnp.bfloat16)
    return high, (value - high.astype(jnp.float32)).astype(jnp.bfloat16)


def dot3(left, right):
    mul = partial(jnp.dot, preferred_element_type=jnp.float32)
    return mul(left[0], right[0]) + (mul(left[0], right[1]) + mul(left[1], right[0]))


def short_transform(values, orient):
    count = len(values)
    if count == 1:
        return values
    even = short_transform(values[0::2], orient)
    odd = short_transform(values[1::2], orient)
    first, second = [], []
    for at in range(count // 2):
        cosine = math.cos(2.0 * math.pi * at / count)
        sine = orient * math.sin(2.0 * math.pi * at / count)
        real, imag = odd[at]
        if at == 0:
            spun = (real, imag)
        elif 4 * at == count:
            spun = (-orient * imag, orient * real)
        else:
            spun = (real * cosine - imag * sine, real * sine + imag * cosine)
        first.append(plus(even[at], spun))
        second.append((even[at][0] - spun[0], even[at][1] - spun[1]))
    return first + second


def fused_kernel(
    sizes,
    x_ref,
    dft_hbm,
    kern_hbm,
    base_hbm,
    spin_hbm,
    final_hbm,
    out_ref,
    dft,
    kern,
    base,
    spin,
    final,
    gathered,
    total,
    data_high,
    data_low,
    send_block,
    recv_block,
    send_tail,
    recv_tail,
    post,
    twist,
    table_sem,
    gather_send,
    gather_recv,
    block_send,
    block_recv,
    tail_send,
    tail_recv,
):
    side, fast_len, fast_local, rows, groups, (cols, subs) = sizes
    points = side * side
    ext = rows * points
    low_len = side // fast_len
    half = low_len * fast_local
    piece = side * low_len // CHUNKS
    members = rows * groups
    row = lax.axis_index("rows")
    col = lax.axis_index("cols")
    sub = lax.axis_index("sub")
    group = col * subs + sub
    me = row * groups + group

    def place(member):
        inside = lax.rem(member, groups)
        return {
            "rows": lax.div(member, groups),
            "cols": lax.div(inside, subs),
            "sub": lax.rem(inside, subs),
        }

    barrier = pltpu.get_barrier_semaphore()
    for near in ({"cols": 1 - col}, {"sub": 1 - sub}):
        pl.semaphore_signal(barrier, inc=1, device_id=near, device_id_type=MESH)

    @pl.when(row > 0)
    def _():
        pl.semaphore_signal(barrier, inc=1, device_id={"rows": row - 1}, device_id_type=MESH)

    @pl.when(row < rows - 1)
    def _():
        pl.semaphore_signal(barrier, inc=1, device_id={"rows": row + 1}, device_id_type=MESH)

    loads = [
        pltpu.make_async_copy(dft_hbm, dft, table_sem.at[0]),
        pltpu.make_async_copy(base_hbm, base, table_sem.at[1]),
        pltpu.make_async_copy(kern_hbm.at[row], kern, table_sem.at[2]),
        pltpu.make_async_copy(spin_hbm, spin, table_sem.at[3]),
        pltpu.make_async_copy(final_hbm, final, table_sem.at[4]),
    ]
    for load in loads:
        load.start()
    pl.semaphore_wait(
        barrier,
        2 + (row > 0).astype(jnp.int32) + (row < rows - 1).astype(jnp.int32),
    )

    def hop(source, slot, chunk, way, near):
        span = pl.ds(chunk * piece, piece)
        return pltpu.make_async_remote_copy(
            src_ref=source.at[:, :, span],
            dst_ref=gathered.at[slot, col, :, :, span],
            send_sem=gather_send.at[slot, chunk, way],
            recv_sem=gather_recv.at[slot, col, chunk],
            device_id=near,
            device_id_type=MESH,
        )

    def across_arrival(slot, chunk):
        span = pl.ds(chunk * piece, piece)
        return pltpu.make_async_remote_copy(
            src_ref=x_ref.at[:, :, span],
            dst_ref=gathered.at[slot, 1 - col, :, :, span],
            send_sem=gather_send.at[slot, chunk, 2],
            recv_sem=gather_recv.at[slot, 1 - col, chunk],
            device_id={"cols": 1 - col},
            device_id_type=MESH,
        )

    for chunk in range(CHUNKS):

        @pl.when(row < rows - 1)
        def _():
            hop(x_ref, row, chunk, 0, {"rows": row + 1}).start()

        @pl.when(row > 0)
        def _():
            hop(x_ref, row, chunk, 1, {"rows": row - 1}).start()

        hop(x_ref, row, chunk, 2, {"cols": 1 - col}).start()

    own = pltpu.make_async_copy(x_ref, gathered.at[row, col], table_sem.at[5])
    own.start()

    def stacked(values):
        return jnp.concatenate([value for value in values], 0)

    def slices(real, imag):
        return [
            (real[at * fast_local : (at + 1) * fast_local], imag[at * fast_local : (at + 1) * fast_local])
            for at in range(low_len)
        ]

    def lane_transform(real, imag, orient):
        count = real.shape[0]
        data = split(jnp.concatenate([real, imag], 0))
        cosines = dot3(data, (dft[0], dft[1]))
        sines = dot3(data, (dft[2], dft[3]))
        return (
            cosines[:count] - orient * sines[count:],
            cosines[count:] + orient * sines[:count],
        )

    def first_stage(slot, pair):
        values = [
            (
                gathered[slot, pair, 0, :, at * side : (at + 1) * side],
                gathered[slot, pair, 1, :, at * side : (at + 1) * side],
            )
            for at in range(low_len)
        ]
        for at in range(2):
            sums = values[0][at]
            for value in values[1:]:
                sums = sums + value[at]
            total[pair, at] += sums
        values = short_transform(values, 1.0)
        real = stacked([value[0] for value in values])
        imag = stacked([value[1] for value in values])
        real, imag = times((real, imag), (spin[0], spin[1]))
        real, imag = lane_transform(real, imag, 1.0)
        span = pl.ds(pl.multiple_of(slot * half, half), half)
        real, imag = times((real, imag), (base[0, span], base[1, span]))
        high, low = split(real)
        data_high[pair, span, :side] = high
        data_low[pair, span, :side] = low
        high, low = split(imag)
        data_high[pair, span, side:] = high
        data_low[pair, span, side:] = low

    shift = 0.5 / rows - row.astype(jnp.float32) / rows
    at_row = lax.broadcasted_iota(jnp.int32, (half, side), 0)
    at_lane = lax.broadcasted_iota(jnp.int32, (half, side), 1)
    low_freq = at_row // fast_local + low_len * at_lane
    digit = rows * (fast_local * group + at_row % fast_local) + row
    total[...] = jnp.zeros_like(total)
    own.wait()
    loads[0].wait()
    loads[1].wait()
    loads[3].wait()
    first_stage(row, col)
    centred = (low_freq - side * low_len // 2).astype(jnp.float32)
    angle = centred * (shift * (2.0 * math.pi / points))
    turn_cos = jnp.cos(angle)
    turn_sin = jnp.sin(angle)
    for at in range(rows):
        span = slice(at * half, (at + 1) * half)
        post[0, span] = base[0, span] * turn_cos + base[1, span] * turn_sin
        post[1, span] = base[0, span] * turn_sin - base[1, span] * turn_cos
    tail_angle = ((low_freq * (2 * digit - 1)) % (2 * ext)).astype(jnp.float32) * (math.pi / ext)
    twist[0] = jnp.cos(tail_angle)
    twist[1] = jnp.sin(tail_angle)

    def slot_of(step):
        inner = jnp.where(
            step == 1, row - 1, jnp.where(step == 2, row + 1, 2 * rows - 2 - 3 * row)
        )
        outer = jnp.where(row == 0, step, rows - 1 - step)
        slot = jnp.where((row == 0) | (row == rows - 1), outer, inner)
        return jnp.where(step == 0, row, slot)

    @pl.loop(1, rows + 1)
    def _(step):
        @pl.when(step < rows)
        def _():
            slot = slot_of(step)
            for chunk in range(CHUNKS):
                hop(x_ref, slot, chunk, 0, {"cols": 1 - col}).wait_recv()

                @pl.when((slot < row) & (row < rows - 1))
                def _():
                    hop(gathered.at[slot, col], slot, chunk, 0, {"rows": row + 1}).start()

                @pl.when((slot > row) & (row > 0))
                def _():
                    hop(gathered.at[slot, col], slot, chunk, 1, {"rows": row - 1}).start()

                hop(gathered.at[slot, col], slot, chunk, 2, {"cols": 1 - col}).start()
            first_stage(slot, col)

        before = slot_of(step - 1)
        for chunk in range(CHUNKS):
            across_arrival(before, chunk).wait_recv()
        first_stage(before, 1 - col)

    half_turn = jnp.zeros((1, 1), jnp.float32) + shift * math.pi
    half_cos = jnp.cos(half_turn)
    half_sin = jnp.sin(half_turn)
    mine = subs * half
    row_at = lax.broadcasted_iota(jnp.int32, (mine, side), 0)
    lane_at = lax.broadcasted_iota(jnp.int32, (mine, side), 1)
    constant = (lane_at == 0) & (row_at % half < fast_local)
    parity = jnp.where(constant, (1 - 2 * (row_at % 2)).astype(jnp.float32), 0.0)
    side_at = lax.broadcasted_iota(jnp.int32, (8, side), 1)
    span = pl.ds(pl.multiple_of(col * mine, mine), mine)
    loads[2].wait()

    def block_copy(pair, origin):
        return pltpu.make_async_remote_copy(
            src_ref=send_block.at[pair, 1 - sub],
            dst_ref=recv_block.at[pair * subs + origin],
            send_sem=block_send.at[pair],
            recv_sem=block_recv.at[pair * subs + origin],
            device_id={"sub": 1 - sub},
            device_id_type=MESH,
        )

    for pair in range(cols):
        mean_a, mean_b = (
            jnp.sum(jnp.sum(total[pair, at], 0, keepdims=True), 1, keepdims=True)
            * (1.0 / points)
            for at in range(2)
        )
        moved = dot3((kern[0, span], kern[1, span]), (data_high[pair], data_low[pair]))
        real, imag = times((moved[:, :side], moved[:, side:]), (post[0, span], post[1, span]))
        real = real - parity * (mean_a * half_cos + mean_b * half_sin)
        imag = imag - parity * (mean_b * half_cos - mean_a * half_sin)
        means = jnp.where(side_at < side // 2, mean_a, mean_b)
        real, imag = lane_transform(real, imag, -1.0)
        for at in range(subs):
            values = times(
                (real[at * half : (at + 1) * half], imag[at * half : (at + 1) * half]),
                (spin[0], -spin[1]),
            )
            values = short_transform(slices(*values), -1.0)
            for low in range(low_len):
                for part in range(2):
                    start = part * half + low * fast_local
                    send_block[pair, at, start : start + fast_local] = values[low][part]
            send_block[pair, at, 2 * half :] = means
        block_copy(pair, sub).start()
        recv_block[pair * subs + sub] = send_block[pair, sub]
    for pair in range(cols):
        block_copy(pair, 1 - sub).wait_recv()

    flip = (1 - 2 * (at_row % 2)).astype(jnp.float32)
    part_cos = flip * half_cos
    part_sin = flip * half_sin

    def value(number):
        block, at = divmod(number, 2)
        data = recv_block[block, at * half : (at + 1) * half]
        lane_from = at * (side // 2)
        mean = recv_block[block, 2 * half : 2 * half + 1, lane_from : lane_from + 1]
        return (mean + part_cos * data, part_sin * data)

    wire_a = value(0)
    wire_b = value(1)
    wire_c = value(2)
    gate = times(times(times(value(3), wire_a), wire_b), wire_c)
    gate = plus(gate, times(value(4), wire_a))
    gate = plus(gate, times(value(5), wire_b))
    gate = plus(gate, times(value(6), wire_c))
    gate = plus(gate, value(7))
    values = short_transform(slices(*gate), 1.0)
    real = stacked([value[0] for value in values])
    imag = stacked([value[1] for value in values])
    real, imag = times((real, imag), (spin[0], spin[1]))
    real, imag = lane_transform(real, imag, 1.0)
    real, imag = times((real, imag), (twist[0], twist[1]))
    loads[4].wait()

    breadth = side * low_len // members
    lane_piece = side // members
    tile_lanes = low_len * lane_piece
    lanes = lax.broadcasted_iota(jnp.int32, (2 * fast_local, tile_lanes), 1)
    for tile in range(side // tile_lanes):
        span = slice(tile * tile_lanes, (tile + 1) * tile_lanes)
        pieces = [
            jnp.concatenate(
                [
                    real[at * fast_local : (at + 1) * fast_local, span],
                    imag[at * fast_local : (at + 1) * fast_local, span],
                ],
                0,
            )
            for at in range(low_len)
        ]
        bit = low_len // 2
        while bit:
            keep = (lanes // (lane_piece * bit)) % 2 == 0
            for at in range(low_len):
                if at & bit == 0:
                    first, second = pieces[at], pieces[at + bit]
                    pieces[at] = jnp.where(keep, first, pltpu.roll(second, lane_piece * bit, 1))
                    pieces[at + bit] = jnp.where(
                        keep, pltpu.roll(first, tile_lanes - lane_piece * bit, 1), second
                    )
            bit //= 2
        for at in range(low_len):
            send_tail[tile * low_len + at] = pieces[at]

    def tail_copy(target, slot):
        return pltpu.make_async_remote_copy(
            src_ref=send_tail.at[target],
            dst_ref=recv_tail.at[slot],
            send_sem=tail_send.at[target],
            recv_sem=tail_recv.at[slot],
            device_id=place(target),
            device_id_type=MESH,
        )

    for step in range(1, members):
        tail_copy(lax.rem(me + step, members), me).start()
    recv_tail[me] = send_tail[me]
    for step in range(1, members):
        source = lax.rem(me + step, members)
        tail_copy(source, source).wait_recv()
    flat = recv_tail[...].reshape(members * 2 * fast_local, breadth)
    result = dot3(split(jnp.transpose(flat)), (final[0], final[1]))
    for at in range(low_len):
        picked = result[at * lane_piece : (at + 1) * lane_piece]
        rows_at = pl.ds(at, lane_piece, stride=low_len)
        out_ref[0, rows_at] = picked[:, : rows * fast_len]
        out_ref[1, rows_at] = picked[:, rows * fast_len :]

    for step in range(1, members):
        target = lax.rem(me + step, members)
        tail_copy(target, me).wait_send()
    for pair in range(cols):
        block_copy(pair, sub).wait_send()
    for chunk in range(CHUNKS):
        for slot in range(rows):

            @pl.when((slot <= row) & (row < rows - 1))
            def _():
                hop(x_ref, slot, chunk, 0, {"rows": row + 1}).wait_send()

            @pl.when((slot >= row) & (row > 0))
            def _():
                hop(x_ref, slot, chunk, 1, {"rows": row - 1}).wait_send()

            hop(x_ref, slot, chunk, 2, {"cols": 1 - col}).wait_send()


def fused_on_device(sizes, trace):
    side, fast_len, fast_local, rows, groups, (cols, subs) = sizes
    low_len = side // fast_len
    half = low_len * fast_local
    members = rows * groups
    tables = [jnp.asarray(table) for table in fused_tables(sizes)]
    block = jnp.transpose(trace, (0, 2, 1))
    vmem = pltpu.VMEM
    bf16 = jnp.bfloat16
    f32 = jnp.float32
    dma = pltpu.SemaphoreType.DMA
    breadth = side * low_len // members
    return pl.pallas_call(
        partial(fused_kernel, sizes),
        out_shape=jax.ShapeDtypeStruct((2, breadth, rows * fast_len), f32),
        in_specs=[pl.BlockSpec(memory_space=pltpu.HBM)] * (1 + len(tables)),
        out_specs=pl.BlockSpec(memory_space=vmem),
        scratch_shapes=[
            vmem((4, side, side), bf16),
            vmem((2, side, side), bf16),
            vmem((2, side, side), f32),
            vmem((2, half, side), f32),
            vmem((2, members * 2 * fast_local, 2 * rows * fast_len), bf16),
            vmem((rows, cols) + block.shape, f32),
            vmem((cols, 2, fast_local, side), f32),
            vmem((cols, side, 2 * side), bf16),
            vmem((cols, side, 2 * side), bf16),
            vmem((cols, subs, 2 * half + 8, side), f32),
            vmem((groups, 2 * half + 8, side), f32),
            vmem((members, 2 * fast_local, breadth), f32),
            vmem((members, 2 * fast_local, breadth), f32),
            vmem((2, side, side), f32),
            vmem((2, half, side), f32),
            dma((6,)),
            dma((rows, CHUNKS, 3)),
            dma((rows, cols, CHUNKS)),
            dma((cols,)),
            dma((groups,)),
            dma((members,)),
            dma((members,)),
        ],
        compiler_params=pltpu.CompilerParams(
            collective_id=0, has_side_effects=True, vmem_limit_bytes=67043328 - 288 * 1024
        ),
    )(block, *tables)


def fused_sizes(mesh, trace):
    shape = mesh.shape
    rows = shape["rows"]
    groups = shape["cols"] * shape["sub"]
    slow_len = trace.shape[1] // shape["groups"]
    fast_len = trace.shape[2]
    side = math.isqrt(slow_len * fast_len)
    fast_local = fast_len // rows
    local_cols = trace.shape[0] // groups
    low_len = side // fast_len
    fits = (
        side * side == slow_len * fast_len
        and low_len * fast_len == side
        and rows == 4
        and groups == rows
        and shape["cols"] == 2
        and shape["sub"] == 2
        and local_cols == 2
        and fast_local == 8
        and 2 * low_len * fast_local == 128
        and rows * groups == 2 * low_len
    )
    return (side, fast_len, fast_local, rows, groups, (shape["cols"], shape["sub"])) if fits else None


def solution(mesh):
    placed = (P(("cols", "sub"), "groups", "rows"),)

    def whole(trace):
        sizes = fused_sizes(mesh, trace)
        return jax.shard_map(
            on_device if sizes is None else partial(fused_on_device, sizes),
            mesh=mesh,
            in_specs=placed,
            out_specs=P("groups", ("rows", "cols", "sub"), None),
            check_vma=False,
        )(trace)

    return whole
```

```python
from functools import partial
import math

import jax
import jax.numpy as jnp
import numpy as np
from jax import lax
from jax.experimental import pallas as pl
from jax.experimental.pallas import tpu as pltpu
from jax.sharding import PartitionSpec as P


def dft_table(extent, orient):
    points = jnp.arange(extent, dtype=jnp.int32)
    product = points[:, None] * points[None, :] % extent
    angles = product.astype(jnp.float32) * (orient * 2.0 * math.pi / extent)
    return (jnp.cos(angles), jnp.sin(angles))


def complex_apply(table_real, table_imag, data_real, data_imag):
    matmul = partial(jnp.dot, precision=lax.Precision.HIGHEST, preferred_element_type=jnp.float32)
    out_real = matmul(table_real, data_real) - matmul(table_imag, data_imag)
    out_imag = matmul(table_real, data_imag) + matmul(table_imag, data_real)
    return (out_real, out_imag)


def rotate(data_real, data_imag, angles):
    cosine = jnp.cos(angles)
    sine = jnp.sin(angles)
    return (data_real * cosine - data_imag * sine, data_real * sine + data_imag * cosine)


def turn(index_product, modulus, orient):
    return (index_product % modulus).astype(jnp.float32) * (orient * 2.0 * math.pi / modulus)


def transform_lead(data_real, data_imag, orient):
    extent = data_real.shape[0]
    rest_shape = data_real.shape[1:]
    breadth = data_real.size // extent
    flat_real = data_real.reshape(extent, breadth)
    flat_imag = data_imag.reshape(extent, breadth)
    if extent <= 128:
        table_real, table_imag = dft_table(extent, orient)
        out_real, out_imag = complex_apply(table_real, table_imag, flat_real, flat_imag)
    else:
        outer_len = extent // 128
        first_real, first_imag = transform_lead(
            flat_real.reshape(outer_len, 128 * breadth),
            flat_imag.reshape(outer_len, 128 * breadth),
            orient,
        )
        first_real = first_real.reshape(outer_len, 128, breadth)
        first_imag = first_imag.reshape(outer_len, 128, breadth)
        outer_index = jnp.arange(outer_len, dtype=jnp.int32)[:, None]
        inner_index = jnp.arange(128, dtype=jnp.int32)[None, :]
        angles = turn(outer_index * inner_index, extent, orient)[:, :, None]
        first_real, first_imag = rotate(first_real, first_imag, angles)
        first_real = jnp.transpose(first_real, (1, 0, 2)).reshape(128, outer_len * breadth)
        first_imag = jnp.transpose(first_imag, (1, 0, 2)).reshape(128, outer_len * breadth)
        out_real, out_imag = transform_lead(first_real, first_imag, orient)
    return (out_real.reshape((extent,) + rest_shape), out_imag.reshape((extent,) + rest_shape))


def times(first, second):
    return (
        first[0] * second[0] - first[1] * second[1],
        first[0] * second[1] + first[1] * second[0],
    )


def plus(first, second):
    return (first[0] + second[0], first[1] + second[1])


def on_device(trace):
    local_cols = trace.shape[0]
    slow_len = trace.shape[1]
    fast_local = trace.shape[2]
    row_parts = lax.axis_size("rows")
    group_parts = lax.axis_size(("cols", "sub"))
    row_index = lax.axis_index("rows")
    group_index = lax.axis_index(("cols", "sub"))
    fast_len = fast_local * row_parts
    trace_len = slow_len * fast_len
    ext_len = 4 * trace_len
    ext_slow = 4 * fast_len
    slow_block = slow_len // row_parts
    ext_block = ext_slow // row_parts
    point_block = ext_block // group_parts
    coeff_block = slow_block // group_parts
    real_part = jnp.transpose(trace, (1, 0, 2))
    imag_part = jnp.zeros_like(real_part)
    real_part, imag_part = transform_lead(real_part, imag_part, 1.0)
    lead_index = jnp.arange(slow_len, dtype=jnp.int32)[:, None, None]
    fast_index = (row_index * fast_local + jnp.arange(fast_local, dtype=jnp.int32))[None, None, :]
    real_part, imag_part = rotate(
        real_part, imag_part, turn(lead_index * fast_index, trace_len, 1.0)
    )
    moved = lax.all_to_all(
        jnp.stack([real_part, imag_part]), "rows", split_axis=1, concat_axis=3, tiled=True
    )
    moved = jnp.transpose(moved, (0, 3, 2, 1))
    real_part, imag_part = transform_lead(moved[0], moved[1], 1.0)
    slow_index = (row_index * slow_block + jnp.arange(slow_block, dtype=jnp.int32))[None, None, :]
    coeff_index = jnp.arange(fast_len, dtype=jnp.int32)[:, None, None] * slow_len + slow_index
    shift_angle = coeff_index.astype(jnp.float32) * (math.pi / (4.0 * trace_len))
    real_part, imag_part = rotate(real_part / trace_len, imag_part / trace_len, shift_angle)
    padding = jnp.zeros((ext_slow - fast_len, local_cols, slow_index.shape[2]), jnp.float32)
    real_part = jnp.concatenate([real_part, padding], 0)
    imag_part = jnp.concatenate([imag_part, padding], 0)
    real_part, imag_part = transform_lead(real_part, imag_part, -1.0)
    ext_index = jnp.arange(ext_slow, dtype=jnp.int32)[:, None, None]
    real_part, imag_part = rotate(real_part, imag_part, turn(ext_index * slow_index, ext_len, -1.0))
    stacked = jnp.stack([real_part, imag_part])
    moved = lax.all_to_all(stacked, "rows", split_axis=1, concat_axis=3, tiled=True)
    moved = jnp.transpose(moved, (0, 3, 2, 1))
    real_part, imag_part = transform_lead(moved[0], moved[1], -1.0)
    joined = lax.all_to_all(
        jnp.stack([real_part, imag_part]), ("cols", "sub"), split_axis=3, concat_axis=2, tiled=True
    )
    real_part = joined[0]
    imag_part = joined[1]

    def column(number):
        return (real_part[:, number], imag_part[:, number])

    wire_a = column(0)
    wire_b = column(1)
    wire_c = column(2)
    gate = times(times(times(column(3), wire_a), wire_b), wire_c)
    gate = plus(gate, times(column(4), wire_a))
    gate = plus(gate, times(column(5), wire_b))
    gate = plus(gate, times(column(6), wire_c))
    gate = plus(gate, column(7))
    point_index = (
        row_index * ext_block + group_index * point_block + jnp.arange(point_block, dtype=jnp.int32)
    )
    quarter = (point_index % 4).astype(jnp.float32)
    vanish_angle = math.pi / 4.0 - math.pi / 2.0 * quarter
    vanish_real = (jnp.cos(vanish_angle) - 1.0)[None, :]
    vanish_imag = jnp.sin(vanish_angle)[None, :]
    magnitude = vanish_real * vanish_real + vanish_imag * vanish_imag
    ratio_real = (gate[0] * vanish_real + gate[1] * vanish_imag) / magnitude
    ratio_imag = (gate[1] * vanish_real - gate[0] * vanish_imag) / magnitude
    real_part, imag_part = transform_lead(ratio_real, ratio_imag, 1.0)
    freq_index = jnp.arange(slow_len, dtype=jnp.int32)[:, None]
    real_part, imag_part = rotate(
        real_part, imag_part, turn(freq_index * point_index[None, :], ext_len, 1.0)
    )
    moved = lax.all_to_all(
        lax.all_to_all(
            jnp.stack([real_part, imag_part]), "rows", split_axis=1, concat_axis=2, tiled=True
        ),
        ("cols", "sub"),
        split_axis=1,
        concat_axis=2,
        tiled=True,
    )
    moved = moved.reshape(2, coeff_block, group_parts, row_parts, point_block)
    moved = jnp.transpose(moved, (0, 3, 2, 4, 1)).reshape(2, ext_slow, coeff_block)
    real_part, imag_part = transform_lead(moved[0], moved[1], 1.0)
    low_index = (
        row_index * slow_block
        + group_index * coeff_block
        + jnp.arange(coeff_block, dtype=jnp.int32)
    )[None, :]
    final_index = jnp.arange(ext_slow, dtype=jnp.int32)[:, None] * slow_len + low_index
    final_angle = final_index.astype(jnp.float32) * (-math.pi / (4.0 * trace_len))
    real_part, imag_part = rotate(real_part, imag_part, final_angle)
    result = jnp.stack([real_part, imag_part]) * (1.0 / math.sqrt(ext_len))
    return jnp.transpose(result, (0, 2, 1))


MESH = pl.DeviceIdType.MESH
CHUNKS = 4


def halves(table):
    high = table.astype(jnp.bfloat16)
    low = (table - high.astype(np.float64)).astype(jnp.bfloat16)
    return high, low


def fused_tables(sizes):
    side, fast_len, fast_local, rows, groups, blocks = sizes
    points = side * side
    ext = rows * points
    low_len = side // fast_len
    slow_len = side * low_len
    index = np.arange(side)
    angles = 2.0 * np.pi * (index[:, None] * index[None, :] % side) / side
    dft = np.stack(halves(np.cos(angles)) + halves(np.sin(angles)))
    row_at, low_at, fast_at = (
        grid.reshape(-1)
        for grid in np.meshgrid(
            np.arange(rows), np.arange(low_len), np.arange(fast_local), indexing="ij"
        )
    )
    inner = fast_local * row_at + fast_at
    centred = low_at[:, None] + low_len * index[None, :] - slow_len // 2
    theta = 2.0 * np.pi * inner[:, None] * centred / points
    base = np.stack([np.cos(theta), np.sin(theta)]).astype(np.float32)
    shifts = 0.5 / rows - np.arange(rows) / rows
    same = low_at[:, None] == low_at[None, :]
    sign = 1.0 - 2.0 * (inner[:, None] % 2)
    kernels = []
    for shift in shifts:
        gap = inner[None, :] - inner[:, None] + shift
        weight = sign / points * np.sin(np.pi * shift) / np.sin(np.pi * gap / fast_len)
        kernels.append(np.stack(halves(np.where(same, weight, 0.0))))
    kernels = np.stack(kernels)
    low_index = np.repeat(np.arange(low_len), fast_local)
    spin = 2.0 * np.pi * low_index[:, None] * index[None, :] / slow_len
    spin = np.stack([np.cos(spin), np.sin(spin)]).astype(np.float32)
    source_row, source_group, fast_at = np.meshgrid(
        np.arange(rows), np.arange(groups), np.arange(fast_local), indexing="ij"
    )
    low_digit = rows * (fast_local * source_group + fast_at) + source_row
    vanish = np.exp(1j * (np.pi / rows - 2.0 * np.pi / rows * source_row)) - 1.0
    finals = np.arange(rows * fast_len)
    turns = np.exp(
        2j * np.pi * low_digit[..., None] * finals / (rows * fast_len)
        - 1j * np.pi * slow_len * finals / ext
    ) / (vanish[..., None] * math.sqrt(ext))
    real_rows = np.concatenate([turns.real, turns.imag], -1)
    imag_rows = np.concatenate([-turns.imag, turns.real], -1)
    final = np.stack([real_rows, imag_rows], 2).reshape(-1, 2 * rows * fast_len)
    final = np.stack(halves(final))
    return dft, kernels, base, spin, final


def split(value):
    high = value.astype(jnp.bfloat16)
    return high, (value - high.astype(jnp.float32)).astype(jnp.bfloat16)


def dot3(left, right):
    mul = partial(jnp.dot, preferred_element_type=jnp.float32)
    return mul(left[0], right[0]) + (mul(left[0], right[1]) + mul(left[1], right[0]))


def short_transform(values, orient):
    count = len(values)
    if count == 1:
        return values
    even = short_transform(values[0::2], orient)
    odd = short_transform(values[1::2], orient)
    first, second = [], []
    for at in range(count // 2):
        cosine = math.cos(2.0 * math.pi * at / count)
        sine = orient * math.sin(2.0 * math.pi * at / count)
        real, imag = odd[at]
        if at == 0:
            spun = (real, imag)
        elif 4 * at == count:
            spun = (-orient * imag, orient * real)
        else:
            spun = (real * cosine - imag * sine, real * sine + imag * cosine)
        first.append(plus(even[at], spun))
        second.append((even[at][0] - spun[0], even[at][1] - spun[1]))
    return first + second


def fused_kernel(
    sizes,
    x_ref,
    dft_hbm,
    kern_hbm,
    base_hbm,
    spin_hbm,
    final_hbm,
    out_ref,
    dft,
    kern,
    base,
    spin,
    final,
    gathered,
    total,
    data_high,
    data_low,
    send_block,
    recv_block,
    send_tail,
    recv_tail,
    post,
    twist,
    table_sem,
    gather_send,
    gather_recv,
    block_send,
    block_recv,
    tail_send,
    tail_recv,
):
    side, fast_len, fast_local, rows, groups, (cols, subs) = sizes
    points = side * side
    ext = rows * points
    low_len = side // fast_len
    half = low_len * fast_local
    piece = side * low_len // CHUNKS
    members = rows * groups
    row = lax.axis_index("rows")
    col = lax.axis_index("cols")
    sub = lax.axis_index("sub")
    group = col * subs + sub
    me = row * groups + group

    def place(member):
        inside = lax.rem(member, groups)
        return {
            "rows": lax.div(member, groups),
            "cols": lax.div(inside, subs),
            "sub": lax.rem(inside, subs),
        }

    barrier = pltpu.get_barrier_semaphore()
    for near in ({"cols": 1 - col}, {"sub": 1 - sub}):
        pl.semaphore_signal(barrier, inc=1, device_id=near, device_id_type=MESH)

    @pl.when(row > 0)
    def _():
        pl.semaphore_signal(barrier, inc=1, device_id={"rows": row - 1}, device_id_type=MESH)

    @pl.when(row < rows - 1)
    def _():
        pl.semaphore_signal(barrier, inc=1, device_id={"rows": row + 1}, device_id_type=MESH)

    loads = [
        pltpu.make_async_copy(dft_hbm, dft, table_sem.at[0]),
        pltpu.make_async_copy(base_hbm, base, table_sem.at[1]),
        pltpu.make_async_copy(kern_hbm.at[row], kern, table_sem.at[2]),
        pltpu.make_async_copy(spin_hbm, spin, table_sem.at[3]),
        pltpu.make_async_copy(final_hbm, final, table_sem.at[4]),
    ]
    for load in loads:
        load.start()
    pl.semaphore_wait(
        barrier,
        2 + (row > 0).astype(jnp.int32) + (row < rows - 1).astype(jnp.int32),
    )

    def hop(source, slot, chunk, way, near):
        span = pl.ds(chunk * piece, piece)
        return pltpu.make_async_remote_copy(
            src_ref=source.at[:, :, span],
            dst_ref=gathered.at[slot, col, :, :, span],
            send_sem=gather_send.at[slot, chunk, way],
            recv_sem=gather_recv.at[slot, col, chunk],
            device_id=near,
            device_id_type=MESH,
        )

    def across_arrival(slot, chunk):
        span = pl.ds(chunk * piece, piece)
        return pltpu.make_async_remote_copy(
            src_ref=x_ref.at[:, :, span],
            dst_ref=gathered.at[slot, 1 - col, :, :, span],
            send_sem=gather_send.at[slot, chunk, 2],
            recv_sem=gather_recv.at[slot, 1 - col, chunk],
            device_id={"cols": 1 - col},
            device_id_type=MESH,
        )

    for chunk in range(CHUNKS):

        @pl.when(row < rows - 1)
        def _():
            hop(x_ref, row, chunk, 0, {"rows": row + 1}).start()

        @pl.when(row > 0)
        def _():
            hop(x_ref, row, chunk, 1, {"rows": row - 1}).start()

        hop(x_ref, row, chunk, 2, {"cols": 1 - col}).start()

    own = pltpu.make_async_copy(x_ref, gathered.at[row, col], table_sem.at[5])
    own.start()

    def stacked(values):
        return jnp.concatenate([value for value in values], 0)

    def slices(real, imag):
        return [
            (real[at * fast_local : (at + 1) * fast_local], imag[at * fast_local : (at + 1) * fast_local])
            for at in range(low_len)
        ]

    def lane_transform(real, imag, orient):
        count = real.shape[0]
        data = split(jnp.concatenate([real, imag], 0))
        cosines = dot3(data, (dft[0], dft[1]))
        sines = dot3(data, (dft[2], dft[3]))
        return (
            cosines[:count] - orient * sines[count:],
            cosines[count:] + orient * sines[:count],
        )

    def first_stage(slot, pair):
        values = [
            (
                gathered[slot, pair, 0, :, at * side : (at + 1) * side],
                gathered[slot, pair, 1, :, at * side : (at + 1) * side],
            )
            for at in range(low_len)
        ]
        for at in range(2):
            sums = values[0][at]
            for value in values[1:]:
                sums = sums + value[at]
            total[pair, at] += sums
        values = short_transform(values, 1.0)
        real = stacked([value[0] for value in values])
        imag = stacked([value[1] for value in values])
        real, imag = times((real, imag), (spin[0], spin[1]))
        real, imag = lane_transform(real, imag, 1.0)
        span = pl.ds(pl.multiple_of(slot * half, half), half)
        real, imag = times((real, imag), (base[0, span], base[1, span]))
        high, low = split(real)
        data_high[pair, span, :side] = high
        data_low[pair, span, :side] = low
        high, low = split(imag)
        data_high[pair, span, side:] = high
        data_low[pair, span, side:] = low

    shift = 0.5 / rows - row.astype(jnp.float32) / rows
    at_row = lax.broadcasted_iota(jnp.int32, (half, side), 0)
    at_lane = lax.broadcasted_iota(jnp.int32, (half, side), 1)
    low_freq = at_row // fast_local + low_len * at_lane
    digit = rows * (fast_local * group + at_row % fast_local) + row
    inner = (row > 0) & (row < rows - 1)
    first = jnp.where(row == 0, 1, jnp.where(row == rows - 1, rows - 2, rows - 1 - row))
    end = jnp.where(2 * row < rows, 0, rows - 1)
    far = rows - 1 - end
    near_far = jnp.where(end == 0, rows - 2, 1)
    second = jnp.where(inner, far, near_far)
    third = jnp.where(inner, end, far)

    def relay(slot, chunk):
        hop(x_ref, slot, chunk, 0, {"cols": 1 - col}).wait_recv()

        @pl.when((slot < row) & (row < rows - 1))
        def _():
            hop(gathered.at[slot, col], slot, chunk, 0, {"rows": row + 1}).start()

        @pl.when((slot > row) & (row > 0))
        def _():
            hop(gathered.at[slot, col], slot, chunk, 1, {"rows": row - 1}).start()

        hop(gathered.at[slot, col], slot, chunk, 2, {"cols": 1 - col}).start()

    def relay_near(chunk):
        relay(first, chunk)

        @pl.when(inner)
        def _():
            relay(third, chunk)

    def across(slot):
        for chunk in range(CHUNKS):
            across_arrival(slot, chunk).wait_recv()
        first_stage(slot, 1 - col)

    total[...] = jnp.zeros_like(total)
    own.wait()
    loads[0].wait()
    loads[1].wait()
    loads[3].wait()
    middle = CHUNKS // 2
    for chunk in range(middle):
        relay_near(chunk)
    first_stage(row, col)
    for chunk in range(middle, CHUNKS):
        relay_near(chunk)
    centred = (low_freq - side * low_len // 2).astype(jnp.float32)
    angle = centred * (shift * (2.0 * math.pi / points))
    turn_cos = jnp.cos(angle)
    turn_sin = jnp.sin(angle)
    for at in range(rows):
        span = slice(at * half, (at + 1) * half)
        post[0, span] = base[0, span] * turn_cos + base[1, span] * turn_sin
        post[1, span] = base[0, span] * turn_sin - base[1, span] * turn_cos
    for chunk in range(middle):
        relay(second, chunk)
    tail_angle = ((low_freq * (2 * digit - 1)) % (2 * ext)).astype(jnp.float32) * (math.pi / ext)
    twist[0] = jnp.cos(tail_angle)
    twist[1] = jnp.sin(tail_angle)
    for chunk in range(middle, CHUNKS):
        relay(second, chunk)
    first_stage(first, col)
    across(row)
    for chunk in range(CHUNKS):

        @pl.when(jnp.logical_not(inner))
        def _():
            relay(third, chunk)

    first_stage(second, col)
    across(first)
    first_stage(third, col)
    across(second)
    across(third)

    half_turn = jnp.zeros((1, 1), jnp.float32) + shift * math.pi
    half_cos = jnp.cos(half_turn)
    half_sin = jnp.sin(half_turn)
    mine = subs * half
    row_at = lax.broadcasted_iota(jnp.int32, (mine, side), 0)
    lane_at = lax.broadcasted_iota(jnp.int32, (mine, side), 1)
    constant = (lane_at == 0) & (row_at % half < fast_local)
    parity = jnp.where(constant, (1 - 2 * (row_at % 2)).astype(jnp.float32), 0.0)
    side_at = lax.broadcasted_iota(jnp.int32, (8, side), 1)
    span = pl.ds(pl.multiple_of(col * mine, mine), mine)
    loads[2].wait()

    def block_copy(pair, origin):
        return pltpu.make_async_remote_copy(
            src_ref=send_block.at[pair, 1 - sub],
            dst_ref=recv_block.at[pair * subs + origin],
            send_sem=block_send.at[pair],
            recv_sem=block_recv.at[pair * subs + origin],
            device_id={"sub": 1 - sub},
            device_id_type=MESH,
        )

    for pair in range(cols):
        mean_a, mean_b = (
            jnp.sum(jnp.sum(total[pair, at], 0, keepdims=True), 1, keepdims=True)
            * (1.0 / points)
            for at in range(2)
        )
        moved = dot3((kern[0, span], kern[1, span]), (data_high[pair], data_low[pair]))
        real, imag = times((moved[:, :side], moved[:, side:]), (post[0, span], post[1, span]))
        real = real - parity * (mean_a * half_cos + mean_b * half_sin)
        imag = imag - parity * (mean_b * half_cos - mean_a * half_sin)
        means = jnp.where(side_at < side // 2, mean_a, mean_b)
        real, imag = lane_transform(real, imag, -1.0)
        for at in range(subs):
            values = times(
                (real[at * half : (at + 1) * half], imag[at * half : (at + 1) * half]),
                (spin[0], -spin[1]),
            )
            values = short_transform(slices(*values), -1.0)
            for low in range(low_len):
                for part in range(2):
                    start = part * half + low * fast_local
                    send_block[pair, at, start : start + fast_local] = values[low][part]
            send_block[pair, at, 2 * half :] = means
        block_copy(pair, sub).start()
        recv_block[pair * subs + sub] = send_block[pair, sub]
    for pair in range(cols):
        block_copy(pair, 1 - sub).wait_recv()

    flip = (1 - 2 * (at_row % 2)).astype(jnp.float32)
    part_cos = flip * half_cos
    part_sin = flip * half_sin

    def value(number):
        block, at = divmod(number, 2)
        data = recv_block[block, at * half : (at + 1) * half]
        lane_from = at * (side // 2)
        mean = recv_block[block, 2 * half : 2 * half + 1, lane_from : lane_from + 1]
        return (mean + part_cos * data, part_sin * data)

    wire_a = value(0)
    wire_b = value(1)
    wire_c = value(2)
    gate = times(times(times(value(3), wire_a), wire_b), wire_c)
    gate = plus(gate, times(value(4), wire_a))
    gate = plus(gate, times(value(5), wire_b))
    gate = plus(gate, times(value(6), wire_c))
    gate = plus(gate, value(7))
    values = short_transform(slices(*gate), 1.0)
    real = stacked([value[0] for value in values])
    imag = stacked([value[1] for value in values])
    real, imag = times((real, imag), (spin[0], spin[1]))
    real, imag = lane_transform(real, imag, 1.0)
    real, imag = times((real, imag), (twist[0], twist[1]))
    loads[4].wait()

    breadth = side * low_len // members
    lane_piece = side // members
    tile_lanes = low_len * lane_piece
    lanes = lax.broadcasted_iota(jnp.int32, (2 * fast_local, tile_lanes), 1)
    for tile in range(side // tile_lanes):
        span = slice(tile * tile_lanes, (tile + 1) * tile_lanes)
        pieces = [
            jnp.concatenate(
                [
                    real[at * fast_local : (at + 1) * fast_local, span],
                    imag[at * fast_local : (at + 1) * fast_local, span],
                ],
                0,
            )
            for at in range(low_len)
        ]
        bit = low_len // 2
        while bit:
            keep = (lanes // (lane_piece * bit)) % 2 == 0
            for at in range(low_len):
                if at & bit == 0:
                    first, second = pieces[at], pieces[at + bit]
                    pieces[at] = jnp.where(keep, first, pltpu.roll(second, lane_piece * bit, 1))
                    pieces[at + bit] = jnp.where(
                        keep, pltpu.roll(first, tile_lanes - lane_piece * bit, 1), second
                    )
            bit //= 2
        for at in range(low_len):
            send_tail[tile * low_len + at] = pieces[at]

    def tail_copy(target, slot):
        return pltpu.make_async_remote_copy(
            src_ref=send_tail.at[target],
            dst_ref=recv_tail.at[slot],
            send_sem=tail_send.at[target],
            recv_sem=tail_recv.at[slot],
            device_id=place(target),
            device_id_type=MESH,
        )

    for step in range(1, members):
        tail_copy(lax.rem(me + step, members), me).start()
    recv_tail[me] = send_tail[me]
    for step in range(1, members):
        source = lax.rem(me + step, members)
        tail_copy(source, source).wait_recv()
    flat = recv_tail[...].reshape(members * 2 * fast_local, breadth)
    result = dot3(split(jnp.transpose(flat)), (final[0], final[1]))
    for at in range(low_len):
        picked = result[at * lane_piece : (at + 1) * lane_piece]
        rows_at = pl.ds(at, lane_piece, stride=low_len)
        out_ref[0, rows_at] = picked[:, : rows * fast_len]
        out_ref[1, rows_at] = picked[:, rows * fast_len :]

    for step in range(1, members):
        target = lax.rem(me + step, members)
        tail_copy(target, me).wait_send()
    for pair in range(cols):
        block_copy(pair, sub).wait_send()
    for chunk in range(CHUNKS):
        for slot in range(rows):

            @pl.when((slot <= row) & (row < rows - 1))
            def _():
                hop(x_ref, slot, chunk, 0, {"rows": row + 1}).wait_send()

            @pl.when((slot >= row) & (row > 0))
            def _():
                hop(x_ref, slot, chunk, 1, {"rows": row - 1}).wait_send()

            hop(x_ref, slot, chunk, 2, {"cols": 1 - col}).wait_send()


def fused_on_device(sizes, trace):
    side, fast_len, fast_local, rows, groups, (cols, subs) = sizes
    low_len = side // fast_len
    half = low_len * fast_local
    members = rows * groups
    tables = [jnp.asarray(table) for table in fused_tables(sizes)]
    block = jnp.transpose(trace, (0, 2, 1))
    vmem = pltpu.VMEM
    bf16 = jnp.bfloat16
    f32 = jnp.float32
    dma = pltpu.SemaphoreType.DMA
    breadth = side * low_len // members
    return pl.pallas_call(
        partial(fused_kernel, sizes),
        out_shape=jax.ShapeDtypeStruct((2, breadth, rows * fast_len), f32),
        in_specs=[pl.BlockSpec(memory_space=pltpu.HBM)] * (1 + len(tables)),
        out_specs=pl.BlockSpec(memory_space=vmem),
        scratch_shapes=[
            vmem((4, side, side), bf16),
            vmem((2, side, side), bf16),
            vmem((2, side, side), f32),
            vmem((2, half, side), f32),
            vmem((2, members * 2 * fast_local, 2 * rows * fast_len), bf16),
            vmem((rows, cols) + block.shape, f32),
            vmem((cols, 2, fast_local, side), f32),
            vmem((cols, side, 2 * side), bf16),
            vmem((cols, side, 2 * side), bf16),
            vmem((cols, subs, 2 * half + 8, side), f32),
            vmem((groups, 2 * half + 8, side), f32),
            vmem((members, 2 * fast_local, breadth), f32),
            vmem((members, 2 * fast_local, breadth), f32),
            vmem((2, side, side), f32),
            vmem((2, half, side), f32),
            dma((6,)),
            dma((rows, CHUNKS, 3)),
            dma((rows, cols, CHUNKS)),
            dma((cols,)),
            dma((groups,)),
            dma((members,)),
            dma((members,)),
        ],
        compiler_params=pltpu.CompilerParams(
            collective_id=0, has_side_effects=True, vmem_limit_bytes=67043328 - 288 * 1024
        ),
    )(block, *tables)


def fused_sizes(mesh, trace):
    shape = mesh.shape
    rows = shape["rows"]
    groups = shape["cols"] * shape["sub"]
    slow_len = trace.shape[1] // shape["groups"]
    fast_len = trace.shape[2]
    side = math.isqrt(slow_len * fast_len)
    fast_local = fast_len // rows
    local_cols = trace.shape[0] // groups
    low_len = side // fast_len
    fits = (
        side * side == slow_len * fast_len
        and low_len * fast_len == side
        and rows == 4
        and groups == rows
        and shape["cols"] == 2
        and shape["sub"] == 2
        and local_cols == 2
        and fast_local == 8
        and 2 * low_len * fast_local == 128
        and rows * groups == 2 * low_len
    )
    return (side, fast_len, fast_local, rows, groups, (shape["cols"], shape["sub"])) if fits else None


def solution(mesh):
    placed = (P(("cols", "sub"), "groups", "rows"),)

    def whole(trace):
        sizes = fused_sizes(mesh, trace)
        return jax.shard_map(
            on_device if sizes is None else partial(fused_on_device, sizes),
            mesh=mesh,
            in_specs=placed,
            out_specs=P("groups", ("rows", "cols", "sub"), None),
            check_vma=False,
        )(trace)

    return whole
```
